128 devices in a mesh: seq: 16 (over z, x), head: 8 (over y, core).
Axes of the slice: x: 4, y: 4, z: 4, core: 2. Of those that a mesh axis runs over, the one named last changes fastest.
Arguments:
- queries: bfloat16 [16384, 32, 128], P('seq', 'head'), may hold values from -6 to 6
- seg_keys: bfloat16 [16384, 32, 128], P('seq', 'head'), may hold values from -6 to 6
- seg_values: bfloat16 [16384, 32, 128], P('seq', 'head'), may hold values from -6 to 6
- mem_keys: bfloat16 [65536, 32, 128], P('seq', 'head'), may hold values from -6 to 6
- mem_values: bfloat16 [65536, 32, 128], P('seq', 'head'), may hold values from -6 to 6
- mem_blocks: int32 [128, 4], P(('seq', 'head')), may hold values from 0 to 511, as said below
- mem_count: int32 [128], P(('seq', 'head')), may hold values from 1 to 4, as said below
- grad_out: bfloat16 [16384, 32, 128], P('seq', 'head'), may hold values from -6 to 6
Outputs:
- attn_out: bfloat16 [16384, 32, 128], P('seq', 'head')
- grad_q: bfloat16 [16384, 32, 128], P('seq', 'head')
- grad_k: bfloat16 [16384, 32, 128], P('seq', 'head')
- grad_v: bfloat16 [16384, 32, 128], P('seq', 'head')
The draws below stay inside these ranges and needn't reach their ends.
Inputs may be any that keep to these rules, and one draw needn't show every extreme that they name: `mem_blocks`: block n is held by owner n // 32. Among the 32 entries of the 8 query blocks of one seq shard (aligned blocks of 8 rows), at most 4 lie with one owner, and one owner has exactly 4 from every shard. Among the used entries (s < mem_count) of one seq shard at most 2 lie with one owner, and that same owner has exactly 2 used entries from every shard. `mem_count`: the counts of the 8 query blocks of one seq shard (aligned blocks of 8 rows) add up to 20, and in every such block of rows one count is 4.
All inputs are finite; a program needn't handle non-finite values.
Results may differ from the reference program's by a relative error of at most 0.012.
Values may be sent and summed in bfloat16 or wider, within the bound.
A program may use at most 192 MiB of HBM per device.

```python
import math
import jax
import jax.numpy as jnp
from jax import lax

HEADS = 32
HEAD_DIM = 128
WINDOW = 1024
BLOCK = 128
TOPK = 4
MEM_DEV = 32
QB_DEV = 8
TOKENS = 16384
QBLOCKS = 128
OWNERS = 16
MEM_BLOCKS = 512
MEM_TOKENS = 65536
CAP = 4
LIVE_SUM = 20
LIVE_CAP = 2


def drawn_pair(key):
    shape = (TOKENS, HEADS, HEAD_DIM)
    query_draw = jnp.clip(jax.random.normal(jax.random.fold_in(key, 21), shape, jnp.float32), -6.0, 6.0)
    key_draw = jnp.clip(jax.random.normal(jax.random.fold_in(key, 22), shape, jnp.float32), -6.0, 6.0)
    return (query_draw, key_draw)


def draw_queries(key, part):
    return drawn_pair(key)[0].astype(jnp.bfloat16)


def draw_seg_keys(key, part):
    return drawn_pair(key)[1].astype(jnp.bfloat16)


def owner_series(hot_owner, per_owner, total, shuffle_key):
    others = (hot_owner + 1 + jnp.arange((OWNERS - 1) * per_owner, dtype=jnp.int32) // per_owner) % OWNERS
    others = jax.random.permutation(jax.random.fold_in(shuffle_key, 1), others)
    series = jnp.concatenate([jnp.full((per_owner,), hot_owner, jnp.int32), others])[:total]
    return jax.random.permutation(jax.random.fold_in(shuffle_key, 2), series)


def block_plan(key):
    slot_total = QB_DEV * TOPK
    units = QB_DEV * (TOPK - 1)
    extra = LIVE_SUM - QB_DEV
    dead_total = slot_total - LIVE_SUM
    hot_owner = jax.random.randint(jax.random.fold_in(key, 31), (), 0, OWNERS, dtype=jnp.int32)

    def one_shard(shard_id):
        shard_key = jax.random.fold_in(jax.random.fold_in(key, 32), shard_id)
        unit_block = jnp.arange(units, dtype=jnp.int32) // (TOPK - 1)
        full_block = jax.random.randint(jax.random.fold_in(shard_key, 4), (), 0, QB_DEV, dtype=jnp.int32)
        unit_rank = jax.random.permutation(jax.random.fold_in(shard_key, 5), units).astype(jnp.int32)
        unit_rank = jnp.where(unit_block == full_block, -1 - jnp.arange(units, dtype=jnp.int32) % (TOPK - 1), unit_rank)
        picked_order = jnp.argsort(unit_rank)
        chosen = jnp.zeros((units,), jnp.int32).at[picked_order[:extra]].set(1)
        counts = 1 + jnp.sum(chosen.reshape(QB_DEV, TOPK - 1), 1)
        live = (jnp.arange(TOPK, dtype=jnp.int32)[None, :] < counts[:, None]).reshape(-1)
        live_list = owner_series(hot_owner, LIVE_CAP, LIVE_SUM, jax.random.fold_in(shard_key, 6))
        dead_list = owner_series(hot_owner, CAP - LIVE_CAP, dead_total, jax.random.fold_in(shard_key, 7))
        place_rank = jnp.where(live, 0, slot_total) + jnp.arange(slot_total, dtype=jnp.int32)
        place_order = jnp.argsort(place_rank)
        owner_list = jnp.zeros((slot_total,), jnp.int32).at[place_order].set(jnp.concatenate([live_list, dead_list]))
        inside = jax.random.randint(jax.random.fold_in(shard_key, 3), (slot_total,), 0, MEM_DEV, dtype=jnp.int32)
        return ((owner_list * MEM_DEV + inside).reshape(QB_DEV, TOPK), counts.astype(jnp.int32))
    ids, counts = jax.vmap(one_shard)(jnp.arange(OWNERS, dtype=jnp.int32))
    return (ids.reshape(QBLOCKS, TOPK).astype(jnp.int32), counts.reshape(QBLOCKS).astype(jnp.int32))


def draw_mem_blocks(key, part):
    return block_plan(key)[0]


def draw_mem_count(key, part):
    return block_plan(key)[1]


def shard_levels(key, dims, split, least, high):
    gain = 1.0
    for axis_at, parts in split:
        draws = jax.random.uniform(jax.random.fold_in(jax.random.fold_in(key, 6), axis_at), (parts,), jnp.float32, least / len(split), high / len(split))
        gain = gain * jnp.repeat(jnp.exp(draws), dims[axis_at] // parts).reshape((-1,) + (1,) * (len(dims) - 1 - axis_at))
    return gain


def gaussian(key, dims, scale, reach, cuts=(), held_as=jnp.bfloat16):
    level = shard_levels(key, dims, cuts, -0.22, 0.18) if cuts else 1.0
    drawn = jax.random.normal(key, dims, jnp.float32) * scale * level
    return jnp.minimum(jnp.maximum(drawn, -reach), reach).astype(held_as)


def setup_inputs(seed: int = 0) -> dict:
    key_list = jax.random.split(jax.random.key(seed), 9)
    queries = draw_queries(jax.random.fold_in(key_list[8], 71), 0)
    seg_keys = draw_seg_keys(jax.random.fold_in(key_list[8], 71), 0)
    seg_values = gaussian(key_list[2], (TOKENS, HEADS, HEAD_DIM), 1.0, 6.0, ((0, 16), (1, 8)))
    mem_keys = gaussian(key_list[3], (MEM_TOKENS, HEADS, HEAD_DIM), 1.0, 6.0, ((0, 16), (1, 8)))
    mem_values = gaussian(key_list[4], (MEM_TOKENS, HEADS, HEAD_DIM), 1.0, 6.0, ((0, 16), (1, 8)))
    mem_blocks = draw_mem_blocks(jax.random.fold_in(key_list[8], 71), 0)
    mem_count = draw_mem_count(jax.random.fold_in(key_list[8], 71), 0)
    grad_out = gaussian(key_list[7], (TOKENS, HEADS, HEAD_DIM), 1.0, 6.0, ((0, 16), (1, 8)))
    return dict(queries=queries, seg_keys=seg_keys, seg_values=seg_values, mem_keys=mem_keys, mem_values=mem_values, mem_blocks=mem_blocks, mem_count=mem_count, grad_out=grad_out)


def settle(tensor):
    return lax.optimization_barrier(tensor.astype(jnp.bfloat16)).astype(jnp.float32)

def band_mask(query_pos, key_pos):
    gap_size = query_pos[:, None] - key_pos[None, :]
    return (gap_size >= 0) & (gap_size < WINDOW) & (key_pos[None, :] >= 0)

def reference(queries, seg_keys, seg_values, mem_keys, mem_values, mem_blocks, mem_count, grad_out):
    score_scale = 1.0 / math.sqrt(HEAD_DIM)
    span_keys = WINDOW + BLOCK
    mem_span = TOPK * BLOCK
    pad_rows = jnp.zeros((WINDOW, HEADS, HEAD_DIM), seg_keys.dtype)
    keys_padded = jnp.concatenate([pad_rows, seg_keys], 0)
    values_padded = jnp.concatenate([pad_rows, seg_values], 0)
    mem_key_blocks = mem_keys.reshape(MEM_BLOCKS, BLOCK, HEADS, HEAD_DIM)
    mem_value_blocks = mem_values.reshape(MEM_BLOCKS, BLOCK, HEADS, HEAD_DIM)

    def forward_block(block_id):
        row_start = block_id * BLOCK
        query_rows = lax.dynamic_slice_in_dim(queries, row_start, BLOCK, 0).astype(jnp.float32)
        grad_rows = lax.dynamic_slice_in_dim(grad_out, row_start, BLOCK, 0).astype(jnp.float32)
        key_window = lax.dynamic_slice_in_dim(keys_padded, row_start, span_keys, 0)
        value_window = lax.dynamic_slice_in_dim(values_padded, row_start, span_keys, 0)
        block_ids = lax.dynamic_index_in_dim(mem_blocks, block_id, 0, keepdims=False)
        used_count = lax.dynamic_index_in_dim(mem_count, block_id, 0, keepdims=False)
        mem_key_rows = jnp.take(mem_key_blocks, block_ids, axis=0).reshape(mem_span, HEADS, HEAD_DIM)
        mem_value_rows = jnp.take(mem_value_blocks, block_ids, axis=0).reshape(mem_span, HEADS, HEAD_DIM)
        combined_keys = jnp.concatenate([key_window, mem_key_rows], 0).astype(jnp.float32)
        combined_values = jnp.concatenate([value_window, mem_value_rows], 0).astype(jnp.float32)
        query_pos = row_start + jnp.arange(BLOCK, dtype=jnp.int32)
        key_pos = row_start - WINDOW + jnp.arange(span_keys, dtype=jnp.int32)
        mem_live = jnp.arange(mem_span, dtype=jnp.int32) // BLOCK < used_count
        key_live = jnp.concatenate([band_mask(query_pos, key_pos), jnp.broadcast_to(mem_live[None, :], (BLOCK, mem_span))], 1)
        scores = jnp.einsum('qhd,khd->hqk', query_rows, combined_keys) * score_scale
        scores = jnp.where(key_live[None], scores, -jnp.inf)
        row_top = lax.optimization_barrier(jnp.max(scores, -1, keepdims=True))
        log_total = row_top + jnp.log(lax.optimization_barrier(jnp.sum(jnp.exp(scores - row_top), -1, keepdims=True)))
        prob_full = jnp.exp(scores - log_total)
        attn_rows = jnp.einsum('hqk,khd->qhd', settle(prob_full), combined_values).astype(jnp.bfloat16)
        attn_back = lax.optimization_barrier(attn_rows).astype(jnp.float32)
        delta_rows = lax.optimization_barrier(jnp.sum(grad_rows * attn_back, -1))
        dprob = jnp.einsum('qhd,khd->hqk', grad_rows, combined_values)
        score_gradient = settle(prob_full * (dprob - delta_rows.T[:, :, None]))
        grad_rows_q = (score_scale * jnp.einsum('hqk,khd->qhd', score_gradient, combined_keys)).astype(jnp.bfloat16)
        return (attn_rows, grad_rows_q, log_total[:, :, 0].T, delta_rows)
    attn_blocks, gradq_blocks, lse_blocks, delta_blocks = lax.map(forward_block, jnp.arange(QBLOCKS, dtype=jnp.int32))
    attn_out = attn_blocks.reshape(TOKENS, HEADS, HEAD_DIM)
    grad_q = gradq_blocks.reshape(TOKENS, HEADS, HEAD_DIM)
    lse_all = lse_blocks.reshape(TOKENS, HEADS)
    delta_all = delta_blocks.reshape(TOKENS, HEADS)
    query_tail = jnp.zeros((WINDOW, HEADS, HEAD_DIM), queries.dtype)
    queries_padded = jnp.concatenate([queries, query_tail], 0)
    grads_padded = jnp.concatenate([grad_out, query_tail], 0)
    stat_tail = jnp.zeros((WINDOW, HEADS), jnp.float32)
    padded_log_sum_exp = jnp.concatenate([lse_all, stat_tail], 0)
    delta_padded = jnp.concatenate([delta_all, stat_tail], 0)

    def key_block(block_id):
        row_start = block_id * BLOCK
        key_rows = lax.dynamic_slice_in_dim(seg_keys, row_start, BLOCK, 0).astype(jnp.float32)
        value_rows = lax.dynamic_slice_in_dim(seg_values, row_start, BLOCK, 0).astype(jnp.float32)
        query_rows = lax.dynamic_slice_in_dim(queries_padded, row_start, span_keys, 0).astype(jnp.float32)
        grad_rows = lax.dynamic_slice_in_dim(grads_padded, row_start, span_keys, 0).astype(jnp.float32)
        lse_rows = lax.dynamic_slice_in_dim(padded_log_sum_exp, row_start, span_keys, 0)
        delta_rows = lax.dynamic_slice_in_dim(delta_padded, row_start, span_keys, 0)
        query_pos = row_start + jnp.arange(span_keys, dtype=jnp.int32)
        key_pos = row_start + jnp.arange(BLOCK, dtype=jnp.int32)
        key_live = band_mask(query_pos, key_pos) & (query_pos < TOKENS)[:, None]
        scores = jnp.einsum('qhd,khd->hqk', query_rows, key_rows) * score_scale
        prob_full = jnp.where(key_live[None], jnp.exp(scores - lse_rows.T[:, :, None]), 0.0)
        dprob = jnp.einsum('qhd,khd->hqk', grad_rows, value_rows)
        score_gradient = settle(prob_full * (dprob - delta_rows.T[:, :, None]))
        grad_rows_k = (score_scale * jnp.einsum('hqk,qhd->khd', score_gradient, query_rows)).astype(jnp.bfloat16)
        grad_rows_v = jnp.einsum('hqk,qhd->khd', settle(prob_full), grad_rows).astype(jnp.bfloat16)
        return (grad_rows_k, grad_rows_v)
    gradk_blocks, gradv_blocks = lax.map(key_block, jnp.arange(QBLOCKS, dtype=jnp.int32))
    grad_k = gradk_blocks.reshape(TOKENS, HEADS, HEAD_DIM)
    grad_v = gradv_blocks.reshape(TOKENS, HEADS, HEAD_DIM)
    return (attn_out, grad_q, grad_k, grad_v)
```

```python
import functools
import math

import jax
import jax.numpy as jnp
from jax import lax
from jax.experimental import pallas as pl
from jax.experimental.pallas import tpu as pltpu
from jax.sharding import PartitionSpec as P

WINDOW = 1024
BLOCK = 128
TOPK = 4
LIVE = 2
GROUP = 1
TILE = 256
VMEM = 58 * 1024 * 1024
NEG = -1e30
F32 = jnp.float32
BF16 = jnp.bfloat16
NT = (((1,), (1,)), ((), ()))
TN = (((0,), (0,)), ((), ()))


def rows_to_heads(rows, heads):
    out = lax.broadcasted_iota(jnp.int32, (rows, rows), 0)
    src = lax.broadcasted_iota(jnp.int32, (rows, rows), 1)
    per = rows // heads
    return (src == heads * (out % per) + out // per).astype(BF16)


def heads_to_rows(rows, heads):
    out = lax.broadcasted_iota(jnp.int32, (rows, rows), 0)
    src = lax.broadcasted_iota(jnp.int32, (rows, rows), 1)
    per = rows // heads
    return (src == per * (out % heads) + out // heads).astype(BF16)


def dot(a, b, dims=None):
    if dims is None:
        return jnp.dot(a, b, preferred_element_type=F32)
    return lax.dot_general(a, b, dims, preferred_element_type=F32)


def split_heads_body(heads, group, q_ref, d_ref, k_ref, v_ref, qo_ref, do_ref, *kv_refs):
    perm = rows_to_heads(256, heads)
    per = 256 // heads
    for part in range(q_ref.shape[0] // 256):
        src = pl.ds(part * 256, 256)
        dst = pl.ds(part * per, per)
        qd = dot(perm, jnp.concatenate([q_ref[src, :], d_ref[src, :]], 1)).astype(BF16)
        kv = dot(perm, jnp.concatenate([k_ref[src, :], v_ref[src, :]], 1)).astype(BF16)
        for h in range(heads):
            rows = slice(h * per, (h + 1) * per)
            qo_ref[h, dst, :] = qd[rows, :128]
            do_ref[h, dst, :] = qd[rows, 128:]
            kv_refs[h // group][0, h % group, dst, :] = kv[rows, :128]
            kv_refs[h // group][1, h % group, dst, :] = kv[rows, 128:]


def split_heads(q, d, k, v, heads, group):
    rows = q.shape[0]
    tokens = rows // heads
    steps = 4
    n_groups = heads // group
    in_spec = pl.BlockSpec((rows // steps, 128), lambda i: (i, 0))
    hm = pl.BlockSpec((heads, tokens // steps, 128), lambda i: (0, i, 0))
    kv = pl.BlockSpec((2, group, tokens // steps, 128), lambda i: (0, 0, i, 0))
    return pl.pallas_call(
        functools.partial(split_heads_body, heads, group),
        grid=(steps,),
        in_specs=[in_spec] * 4,
        out_specs=[hm, hm] + [kv] * n_groups,
        out_shape=[jax.ShapeDtypeStruct((heads, tokens, 128), BF16)] * 2
        + [jax.ShapeDtypeStruct((2, group, tokens, 128), BF16)] * n_groups,
        cost_estimate=pl.CostEstimate(
            flops=4 * 2 * rows * 256 * 128, bytes_accessed=16 * rows * 128, transcendentals=0
        ),
        compiler_params=pltpu.CompilerParams(vmem_limit_bytes=VMEM),
        name="split_heads",
    )(q, d, k, v)


def pick_body(heads, group, per_step, idx_ref, *refs):
    ins, outs = refs[: 2 * per_step], refs[2 * per_step :]
    perm = rows_to_heads(256, heads)
    per = 256 // heads
    for j in range(per_step):
        k_ref, v_ref = ins[2 * j], ins[2 * j + 1]
        for part in range(BLOCK * heads // 256):
            src = pl.ds(part * 256, 256)
            dst = pl.ds(part * per, per)
            kv = dot(perm, jnp.concatenate([k_ref[0, src, :], v_ref[0, src, :]], 1)).astype(BF16)
            for h in range(heads):
                rows = slice(h * per, (h + 1) * per)
                outs[h // group][j, 0, h % group, dst, :] = kv[rows, :128]
                outs[h // group][j, 1, h % group, dst, :] = kv[rows, 128:]


def pick_blocks(index, mem_k, mem_v, heads, group):
    slots = index.shape[0]
    per_step = 4
    n_groups = heads // group

    def at(j):
        return pl.BlockSpec(
            (1, BLOCK * heads, 128), lambda i, idx, j=j: (idx[i * per_step + j], 0, 0)
        )

    out = pl.BlockSpec((per_step, 2, group, BLOCK, 128), lambda i, idx: (i, 0, 0, 0, 0))
    ins = []
    for _ in range(per_step):
        ins += [mem_k, mem_v]
    return pl.pallas_call(
        functools.partial(pick_body, heads, group, per_step),
        grid_spec=pltpu.PrefetchScalarGridSpec(
            num_scalar_prefetch=1,
            grid=(slots // per_step,),
            in_specs=[at(j // 2) for j in range(2 * per_step)],
            out_specs=[out] * n_groups,
        ),
        out_shape=[jax.ShapeDtypeStruct((slots, 2, group, BLOCK, 128), BF16)] * n_groups,
        cost_estimate=pl.CostEstimate(
            flops=slots * 4 * BLOCK * heads * 256 * 128,
            bytes_accessed=slots * 8 * BLOCK * heads * 128,
            transcendentals=0,
        ),
        compiler_params=pltpu.CompilerParams(vmem_limit_bytes=VMEM),
        name="pick_blocks",
    )(index, *ins)


def attend_body(
    slot_ref, count_ref, rank_ref, q_ref, g_ref, own_ref, halo_ref, mem_ref,
    o_ref, dq_ref, back_ref, keep_ref,
    kx, vx, km, vm, s_ref, dp_ref, p_ref, ds_ref, ka, va,
):
    t = pl.program_id(1)
    span = WINDOW + TILE
    mem_span = TOPK * BLOCK
    total = span + mem_span
    halves = TILE // BLOCK
    scale = 1.0 / math.sqrt(128.0)
    to_two = scale * math.log2(math.e)

    @pl.when(t == 0)
    def _():
        kx[:WINDOW, :] = halo_ref[0, 0]
        kx[WINDOW:, :] = own_ref[0, 0]
        vx[:WINDOW, :] = halo_ref[1, 0]
        vx[WINDOW:, :] = own_ref[1, 0]
        ka[...] = jnp.zeros_like(ka)
        va[...] = jnp.zeros_like(va)

    start = pl.multiple_of(t * TILE, TILE)
    win = pl.ds(start, span)
    q = q_ref[0, pl.ds(start, TILE), :]
    g = g_ref[0, pl.ds(start, TILE), :]

    for half in range(halves):
        for e in range(TOPK):
            slot = slot_ref[(t * halves + half) * TOPK + e]
            km[half, e * BLOCK : (e + 1) * BLOCK, :] = mem_ref[slot, 0, 0]
            vm[half, e * BLOCK : (e + 1) * BLOCK, :] = mem_ref[slot, 1, 0]

    s_ref[:span, :] = dot(kx[win, :], q, NT)
    dp_ref[:span, :] = dot(vx[win, :], g, NT)
    for half in range(halves):
        cols = slice(half * BLOCK, (half + 1) * BLOCK)
        s_ref[span:, cols] = dot(km[half], q[cols], NT)
        dp_ref[span:, cols] = dot(vm[half], g[cols], NT)

    row = lax.broadcasted_iota(jnp.int32, (TILE, TILE), 0)
    col = lax.broadcasted_iota(jnp.int32, (TILE, TILE), 1)
    s_ref[:TILE, :] = jnp.where(row > col, s_ref[:TILE, :], NEG)
    s_ref[WINDOW:span, :] = jnp.where(row <= col, s_ref[WINDOW:span, :], NEG)

    @pl.when(rank_ref[0] == 0)
    def _():
        for c in range(WINDOW // TILE):
            @pl.when(c + t < WINDOW // TILE)
            def _():
                s_ref[c * TILE : (c + 1) * TILE, :] = jnp.full((TILE, TILE), NEG, F32)

    for half in range(halves):
        used = count_ref[t * halves + half]
        for e in range(1, TOPK):
            @pl.when(e >= used)
            def _():
                s_ref[
                    span + e * BLOCK : span + (e + 1) * BLOCK, half * BLOCK : (half + 1) * BLOCK
                ] = jnp.full((BLOCK, BLOCK), NEG, F32)

    steps = total // BLOCK

    def chunk(c):
        return pl.ds(pl.multiple_of(c * BLOCK, BLOCK), BLOCK)

    def fold(x, op):
        return op(x.reshape(BLOCK // 8, 8, TILE), 0)

    def top_step(c, top):
        return jnp.maximum(top, fold(s_ref[chunk(c), :], jnp.max))

    top = lax.fori_loop(0, steps, top_step, jnp.full((8, TILE), NEG, F32), unroll=2)
    top = jnp.max(top, 0, keepdims=True) * to_two

    def exp_step(c, acc):
        e = jnp.exp2(s_ref[chunk(c), :] * to_two - top)
        s_ref[chunk(c), :] = e
        return acc + fold(e, jnp.sum)

    acc = lax.fori_loop(0, steps, exp_step, jnp.zeros((8, TILE), F32), unroll=2)
    inv = 1.0 / jnp.sum(acc, 0, keepdims=True)

    def prob_step(c, acc):
        p = s_ref[chunk(c), :] * inv
        s_ref[chunk(c), :] = p
        p_ref[chunk(c), :] = p.astype(BF16)
        return acc + fold(p * dp_ref[chunk(c), :], jnp.sum)

    acc = lax.fori_loop(0, steps, prob_step, jnp.zeros((8, TILE), F32), unroll=2)
    delta = jnp.sum(acc, 0, keepdims=True)

    def score_step(c, carry):
        ds_ref[chunk(c), :] = (s_ref[chunk(c), :] * (dp_ref[chunk(c), :] - delta)).astype(BF16)
        return carry

    lax.fori_loop(0, steps, score_step, 0, unroll=2)

    o = dot(p_ref[:span, :], vx[win, :], TN)
    dq = dot(ds_ref[:span, :], kx[win, :], TN)
    for half in range(halves):
        cols = slice(half * BLOCK, (half + 1) * BLOCK)
        o_ref[0, cols, :] = (o[cols] + dot(p_ref[span:, cols], vm[half], TN)).astype(BF16)
        dq_ref[0, cols, :] = (
            scale * (dq[cols] + dot(ds_ref[span:, cols], km[half], TN))
        ).astype(BF16)
    va[win, :] += dot(p_ref[:span, :], g)
    ka[win, :] += dot(ds_ref[:span, :], q)

    @pl.when(t == pl.num_programs(1) - 1)
    def _():
        back_ref[0, 0] = (scale * ka[:WINDOW, :]).astype(BF16)
        back_ref[1, 0] = va[:WINDOW, :].astype(BF16)
        keep_ref[0, 0] = scale * ka[WINDOW:, :]
        keep_ref[1, 0] = va[WINDOW:, :]


def attend(slots, counts, rank, q, g, own, halo, mem, first):
    group, tokens = own.shape[1], own.shape[2]
    n_slots = mem.shape[0]
    tiles = tokens // TILE
    span = WINDOW + TILE
    total = span + TOPK * BLOCK
    halves = TILE // BLOCK
    whole = pl.BlockSpec((1, tokens, 128), lambda i, t, *_: (first + i, 0, 0))
    pair = pl.BlockSpec((2, 1, tokens, 128), lambda i, t, *_: (0, i, 0, 0))
    tile = pl.BlockSpec((1, TILE, 128), lambda i, t, *_: (i, t, 0))
    pairs = group * tiles * total * TILE
    return pl.pallas_call(
        attend_body,
        grid_spec=pltpu.PrefetchScalarGridSpec(
            num_scalar_prefetch=3,
            grid=(group, tiles),
            in_specs=[
                whole, whole, pair, pair,
                pl.BlockSpec((n_slots, 2, 1, BLOCK, 128), lambda i, t, *_: (0, 0, i, 0, 0)),
            ],
            out_specs=[tile, tile, pair, pair],
            scratch_shapes=[
                pltpu.VMEM((2 * WINDOW, 128), BF16),
                pltpu.VMEM((2 * WINDOW, 128), BF16),
                pltpu.VMEM((halves, TOPK * BLOCK, 128), BF16),
                pltpu.VMEM((halves, TOPK * BLOCK, 128), BF16),
                pltpu.VMEM((total, TILE), F32),
                pltpu.VMEM((total, TILE), F32),
                pltpu.VMEM((total, TILE), BF16),
                pltpu.VMEM((total, TILE), BF16),
                pltpu.VMEM((2 * WINDOW, 128), F32),
                pltpu.VMEM((2 * WINDOW, 128), F32),
            ],
        ),
        out_shape=[
            jax.ShapeDtypeStruct((group, tokens, 128), BF16),
            jax.ShapeDtypeStruct((group, tokens, 128), BF16),
            jax.ShapeDtypeStruct((2, group, tokens, 128), BF16),
            jax.ShapeDtypeStruct((2, group, tokens, 128), F32),
        ],
        compiler_params=pltpu.CompilerParams(vmem_limit_bytes=VMEM),
        cost_estimate=pl.CostEstimate(
            flops=pairs * 128 * 12, bytes_accessed=group * 6 * 2**20, transcendentals=pairs
        ),
        name="attend",
    )(slots, counts, rank, q, g, own, halo, mem)


def join_body(heads, group, n_groups, *refs):
    o_refs, dq_refs = refs[:n_groups], refs[n_groups : 2 * n_groups]
    keep_refs, back_refs = refs[2 * n_groups : 3 * n_groups], refs[3 * n_groups : 4 * n_groups]
    o_out, dq_out, dk_out, dv_out = refs[4 * n_groups :]
    perm = heads_to_rows(256, heads)
    per = 256 // heads

    def stack(pieces):
        return jnp.concatenate(pieces, 0)

    for part in range(o_out.shape[0] // 256):
        src = slice(part * per, (part + 1) * per)
        dst = slice(part * 256, (part + 1) * 256)
        hs = range(heads)
        o = stack([o_refs[h // group][h % group, src, :] for h in hs])
        dq = stack([dq_refs[h // group][h % group, src, :] for h in hs])
        both = dot(perm, jnp.concatenate([o, dq], 1)).astype(BF16)
        o_out[dst, :] = both[:, :128]
        dq_out[dst, :] = both[:, 128:]
        sums = []
        for kv in range(2):
            sums.append(
                stack(
                    [
                        (
                            keep_refs[h // group][kv, h % group, src, :]
                            + back_refs[h // group][kv, h % group, src, :].astype(F32)
                        ).astype(BF16)
                        for h in hs
                    ]
                )
            )
        both = dot(perm, jnp.concatenate(sums, 1)).astype(BF16)
        dk_out[dst, :] = both[:, :128]
        dv_out[dst, :] = both[:, 128:]


def join_heads(o, dq, keep, back, heads, group):
    n_groups = heads // group
    tokens = o[0].shape[1]
    steps = 4
    hm = pl.BlockSpec((group, tokens // steps, 128), lambda i: (0, i, 0))
    kv = pl.BlockSpec((2, group, tokens // steps, 128), lambda i: (0, 0, i, 0))
    out = pl.BlockSpec((tokens * heads // steps, 128), lambda i: (i, 0))
    return pl.pallas_call(
        functools.partial(join_body, heads, group, n_groups),
        grid=(steps,),
        in_specs=[hm] * (2 * n_groups) + [kv] * (2 * n_groups),
        out_specs=[out] * 4,
        out_shape=[jax.ShapeDtypeStruct((tokens * heads, 128), BF16)] * 4,
        cost_estimate=pl.CostEstimate(
            flops=4 * 2 * tokens * heads * 256 * 128,
            bytes_accessed=24 * tokens * heads * 128,
            transcendentals=0,
        ),
        compiler_params=pltpu.CompilerParams(vmem_limit_bytes=VMEM),
        name="join_heads",
    )(*o, *dq, *keep, *back)


def passed_along(block, axis, distance):
    devices = range(lax.axis_size(axis))
    route = [(i - distance, i) for i in devices if i - distance in devices]
    return lax.ppermute(block, axis, route)


def after(value, earlier):
    return lax.optimization_barrier((value, earlier))


def tables(mem_blocks, mem_count, mem_local, owners):
    packed = jnp.concatenate([mem_blocks, mem_count[:, None]], 1)
    every = lax.all_gather(packed, ("seq", "head"), axis=0, tiled=True)
    me = lax.axis_index("seq")
    rows = every.shape[0] // owners
    entries = rows * TOPK
    ids = every[:, :TOPK].reshape(owners, entries)
    count = every[:, TOPK].reshape(owners, rows)
    used = (
        jnp.arange(TOPK, dtype=jnp.int32)[None, None, :] < count[:, :, None]
    ).reshape(owners, entries)
    owner = ids // mem_local
    inside = ids % mem_local
    earlier = (
        jnp.arange(entries, dtype=jnp.int32)[None, :] < jnp.arange(entries, dtype=jnp.int32)[:, None]
    )
    same = (owner[:, :, None] == owner[:, None, :]) & used[:, None, :] & earlier[None]
    order = jnp.sum(same.astype(jnp.int32), 2)
    wanted = (
        (used & (owner == me))[:, :, None]
        & (order[:, :, None] == jnp.arange(LIVE, dtype=jnp.int32)[None, None, :])
    )
    send = jnp.sum(jnp.where(wanted, inside[:, :, None], 0), 1).reshape(owners * LIVE)
    slot = jnp.where(used, owner * LIVE + order, 0)
    pick = jnp.arange(owners, dtype=jnp.int32) == me
    mine = jnp.sum(jnp.where(pick[:, None], slot, 0), 0).reshape(rows, TOPK)
    my_count = jnp.sum(jnp.where(pick[:, None], count, 0), 0)
    live = jnp.arange(TOPK, dtype=jnp.int32)[None, :] < my_count[:, None]
    mine = jnp.where(live, mine, mine[:, :1]).reshape(entries)
    return send, mine, my_count, me.reshape(1)


def shards(queries, seg_keys, seg_values, mem_keys, mem_values, mem_blocks, mem_count, grad_out):
    tokens, heads, dim = queries.shape
    owners = lax.axis_size("seq")
    mem_local = mem_keys.shape[0] // BLOCK
    group = GROUP
    n_groups = heads // group

    def as_rows(x):
        return x.reshape(x.shape[0] * heads, dim)

    q, g, *own = split_heads(
        as_rows(queries), as_rows(grad_out), as_rows(seg_keys), as_rows(seg_values), heads, group
    )
    halo = [passed_along(x, "seq", 1) for x in own]
    (mem_blocks, mem_count), _ = after((mem_blocks, mem_count), q)
    send, slots, counts, rank = tables(mem_blocks, mem_count, mem_local, owners)
    picked = pick_blocks(
        send,
        mem_keys.reshape(mem_local, BLOCK * heads, dim),
        mem_values.reshape(mem_local, BLOCK * heads, dim),
        heads,
        group,
    )
    o, dq, keep, back = [], [], [], []
    got = []

    def fetch(i, *earlier):
        x, _ = after(picked[i], (halo[i], *earlier))
        x = x.reshape(owners, LIVE, 2, group, BLOCK, dim)
        x = lax.all_to_all(x, "seq", split_axis=0, concat_axis=0, tiled=True)
        got.append(x.reshape(owners * LIVE, 2, group, BLOCK, dim))

    fetch(0)
    for i in range(n_groups):
        if i + 1 < n_groups:
            fetch(i + 1, got[i], *back[: max(i - 1, 0)])
        parts = attend(slots, counts, rank, q, g, own[i], halo[i], got[i], i * group)
        o.append(parts[0])
        dq.append(parts[1])
        keep.append(parts[3])
        back.append(passed_along(parts[2], "seq", -1))
    outs = join_heads(o, dq, keep, back, heads, group)
    return tuple(x.reshape(tokens, heads, dim) for x in outs)


def solution(mesh):
    wide = P("seq", "head", None)
    return jax.shard_map(
        shards,
        mesh=mesh,
        in_specs=(wide, wide, wide, wide, wide, P(("seq", "head"), None), P(("seq", "head")), wide),
        out_specs=(wide, wide, wide, wide),
        check_vma=False,
    )
```

```python
import functools
import math

import jax
import jax.numpy as jnp
from jax import lax
from jax.experimental import pallas as pl
from jax.experimental.pallas import tpu as pltpu
from jax.sharding import PartitionSpec as P

WINDOW = 1024
BLOCK = 128
TOPK = 4
LIVE = 2
TILE = 256
VMEM = 58 * 1024 * 1024
NEG = -1e30
F32 = jnp.float32
BF16 = jnp.bfloat16
NT = (((1,), (1,)), ((), ()))
TN = (((0,), (0,)), ((), ()))


def rows_to_heads(rows, heads):
    out = lax.broadcasted_iota(jnp.int32, (rows, rows), 0)
    src = lax.broadcasted_iota(jnp.int32, (rows, rows), 1)
    per = rows // heads
    return (src == heads * (out % per) + out // per).astype(BF16)


def heads_to_rows(rows, heads):
    out = lax.broadcasted_iota(jnp.int32, (rows, rows), 0)
    src = lax.broadcasted_iota(jnp.int32, (rows, rows), 1)
    per = rows // heads
    return (src == per * (out % heads) + out // heads).astype(BF16)


def dot(a, b, dims=None):
    if dims is None:
        return jnp.dot(a, b, preferred_element_type=F32)
    return lax.dot_general(a, b, dims, preferred_element_type=F32)


def split_heads_body(heads, q_ref, d_ref, k_ref, v_ref, qo_ref, do_ref, kv_ref):
    perm = rows_to_heads(256, heads)
    per = 256 // heads
    for part in range(q_ref.shape[0] // 256):
        src = pl.ds(part * 256, 256)
        dst = pl.ds(part * per, per)
        qd = dot(perm, jnp.concatenate([q_ref[src, :], d_ref[src, :]], 1)).astype(BF16)
        kv = dot(perm, jnp.concatenate([k_ref[src, :], v_ref[src, :]], 1)).astype(BF16)
        for h in range(heads):
            rows = slice(h * per, (h + 1) * per)
            qo_ref[h, dst, :] = qd[rows, :128]
            do_ref[h, dst, :] = qd[rows, 128:]
            kv_ref[h, 0, dst, :] = kv[rows, :128]
            kv_ref[h, 1, dst, :] = kv[rows, 128:]


def split_heads(q, d, k, v, heads):
    rows = q.shape[0]
    tokens = rows // heads
    steps = 4
    in_spec = pl.BlockSpec((rows // steps, 128), lambda i: (i, 0))
    hm = pl.BlockSpec((heads, tokens // steps, 128), lambda i: (0, i, 0))
    kv = pl.BlockSpec((heads, 2, tokens // steps, 128), lambda i: (0, 0, i, 0))
    return pl.pallas_call(
        functools.partial(split_heads_body, heads),
        grid=(steps,),
        in_specs=[in_spec] * 4,
        out_specs=[hm, hm, kv],
        out_shape=[jax.ShapeDtypeStruct((heads, tokens, 128), BF16)] * 2
        + [jax.ShapeDtypeStruct((heads, 2, tokens, 128), BF16)],
        cost_estimate=pl.CostEstimate(
            flops=4 * 2 * rows * 256 * 128, bytes_accessed=16 * rows * 128, transcendentals=0
        ),
        compiler_params=pltpu.CompilerParams(vmem_limit_bytes=VMEM),
        name="split_heads",
    )(q, d, k, v)


def pick_body(heads, per_step, idx_ref, *refs):
    ins, out = refs[: 2 * per_step], refs[2 * per_step]
    perm = rows_to_heads(256, heads)
    per = 256 // heads
    for j in range(per_step):
        k_ref, v_ref = ins[2 * j], ins[2 * j + 1]
        for part in range(BLOCK * heads // 256):
            src = pl.ds(part * 256, 256)
            dst = pl.ds(part * per, per)
            kv = dot(perm, jnp.concatenate([k_ref[0, src, :], v_ref[0, src, :]], 1)).astype(BF16)
            for h in range(heads):
                rows = slice(h * per, (h + 1) * per)
                out[h, j, 0, dst, :] = kv[rows, :128]
                out[h, j, 1, dst, :] = kv[rows, 128:]


def pick_blocks(index, mem_k, mem_v, heads):
    slots = index.shape[0]
    per_step = 4

    def at(j):
        return pl.BlockSpec(
            (1, BLOCK * heads, 128), lambda i, idx, j=j: (idx[i * per_step + j], 0, 0)
        )

    ins = []
    for _ in range(per_step):
        ins += [mem_k, mem_v]
    return pl.pallas_call(
        functools.partial(pick_body, heads, per_step),
        grid_spec=pltpu.PrefetchScalarGridSpec(
            num_scalar_prefetch=1,
            grid=(slots // per_step,),
            in_specs=[at(j // 2) for j in range(2 * per_step)],
            out_specs=pl.BlockSpec((heads, per_step, 2, BLOCK, 128), lambda i, idx: (0, i, 0, 0, 0)),
        ),
        out_shape=jax.ShapeDtypeStruct((heads, slots, 2, BLOCK, 128), BF16),
        compiler_params=pltpu.CompilerParams(vmem_limit_bytes=VMEM),
        cost_estimate=pl.CostEstimate(
            flops=slots * 4 * BLOCK * heads * 256 * 128,
            bytes_accessed=slots * 8 * BLOCK * heads * 128,
            transcendentals=0,
        ),
        name="pick_blocks",
    )(index, *ins)


def attend_tile(refs, t, rank, h, ka, va):
    (slot_ref, count_ref, q_ref, g_ref, o_ref, dq_ref, cur, kx, vx, km, vm, s_ref, dp_ref, p_ref, ds_ref) = refs
    span = WINDOW + TILE
    total = span + TOPK * BLOCK
    halves = TILE // BLOCK
    scale = 1.0 / math.sqrt(128.0)
    to_two = scale * math.log2(math.e)
    start = pl.multiple_of(t * TILE, TILE)
    win = pl.ds(start, span)
    q = q_ref[h, pl.ds(start, TILE), :]
    g = g_ref[h, pl.ds(start, TILE), :]

    for half in range(halves):
        for e in range(TOPK):
            slot = slot_ref[(t * halves + half) * TOPK + e]
            km[half, e * BLOCK : (e + 1) * BLOCK, :] = cur[slot, 0]
            vm[half, e * BLOCK : (e + 1) * BLOCK, :] = cur[slot, 1]

    s_ref[:span, :] = dot(kx[win, :], q, NT)
    dp_ref[:span, :] = dot(vx[win, :], g, NT)
    for half in range(halves):
        cols = slice(half * BLOCK, (half + 1) * BLOCK)
        used = count_ref[t * halves + half]
        far = dot(km[half], q[cols], NT)
        for e in range(TOPK):
            rows = slice(e * BLOCK, (e + 1) * BLOCK)
            s_ref[span + e * BLOCK : span + (e + 1) * BLOCK, cols] = jnp.where(
                e < used, far[rows], NEG
            )
        dp_ref[span:, cols] = dot(vm[half], g[cols], NT)

    row = lax.broadcasted_iota(jnp.int32, (TILE, TILE), 0)
    col = lax.broadcasted_iota(jnp.int32, (TILE, TILE), 1)
    s_ref[:TILE, :] = jnp.where(row > col, s_ref[:TILE, :], NEG)
    s_ref[WINDOW:span, :] = jnp.where(row <= col, s_ref[WINDOW:span, :], NEG)

    @pl.when(rank == 0)
    def _():
        for c in range(WINDOW // TILE):
            @pl.when(c + t < WINDOW // TILE)
            def _():
                s_ref[c * TILE : (c + 1) * TILE, :] = jnp.full((TILE, TILE), NEG, F32)

    steps = total // BLOCK

    def chunk(c):
        return pl.ds(pl.multiple_of(c * BLOCK, BLOCK), BLOCK)

    def fold(x, op):
        return op(x.reshape(BLOCK // 8, 8, TILE), 0)

    def top_step(c, top):
        return jnp.maximum(top, fold(s_ref[chunk(c), :], jnp.max))

    top = lax.fori_loop(0, steps, top_step, jnp.full((8, TILE), NEG, F32), unroll=2)
    top = jnp.max(top, 0, keepdims=True) * to_two

    def exp_step(c, acc):
        e = jnp.exp2(s_ref[chunk(c), :] * to_two - top)
        s_ref[chunk(c), :] = e
        return acc + fold(e, jnp.sum)

    acc = lax.fori_loop(0, steps, exp_step, jnp.zeros((8, TILE), F32), unroll=2)
    inv = 1.0 / jnp.sum(acc, 0, keepdims=True)

    def prob_step(c, acc):
        p = s_ref[chunk(c), :] * inv
        s_ref[chunk(c), :] = p
        p_ref[chunk(c), :] = p.astype(BF16)
        return acc + fold(p * dp_ref[chunk(c), :], jnp.sum)

    acc = lax.fori_loop(0, steps, prob_step, jnp.zeros((8, TILE), F32), unroll=2)
    delta = jnp.sum(acc, 0, keepdims=True)

    def score_step(c, carry):
        ds_ref[chunk(c), :] = (s_ref[chunk(c), :] * (dp_ref[chunk(c), :] - delta)).astype(BF16)
        return carry

    lax.fori_loop(0, steps, score_step, 0, unroll=2)

    o = dot(p_ref[:span, :], vx[win, :], TN)
    dq = dot(ds_ref[:span, :], kx[win, :], TN)
    for half in range(halves):
        cols = slice(half * BLOCK, (half + 1) * BLOCK)
        dst = pl.ds(pl.multiple_of(start + half * BLOCK, BLOCK), BLOCK)
        o_ref[h, dst, :] = (o[cols] + dot(p_ref[span:, cols], vm[half], TN)).astype(BF16)
        dq_ref[h, dst, :] = (
            scale * (dq[cols] + dot(ds_ref[span:, cols], km[half], TN))
        ).astype(BF16)
    va[win, :] += dot(p_ref[:span, :], g)
    ka[win, :] += dot(ds_ref[:span, :], q)


def exchange_body(
    heads, n, slot_ref, count_ref, q_ref, g_ref, own_ref, sent_ref, o_ref, dq_ref, dkv_ref,
    recv, halo, leave, back, cur, kx, vx, km, vm, s_ref, dp_ref, p_ref, ds_ref, ka, va,
    far_send, far_recv, near, halo_send, halo_recv, back_send, back_recv,
):
    me = lax.axis_index("seq")
    tiles = WINDOW // TILE
    scale = 1.0 / math.sqrt(128.0)
    barrier = pltpu.get_barrier_semaphore()

    def peer(r):
        return lax.rem(me + r, n)

    def greet(r, c):
        pl.semaphore_signal(barrier, inc=1, device_id={"seq": peer(r)})
        return c

    lax.fori_loop(1, n, greet, 0)
    pl.semaphore_wait(barrier, n - 1)

    def far_copy(h, r):
        return pltpu.make_async_remote_copy(
            src_ref=sent_ref.at[h, peer(r)],
            dst_ref=recv.at[h, me],
            send_sem=far_send.at[h, r],
            recv_sem=far_recv.at[h, r],
            device_id={"seq": peer(r)},
        )

    def near_copy(h):
        return pltpu.make_async_copy(sent_ref.at[h, me], recv.at[h, me], near.at[h])

    def halo_copy(h):
        return pltpu.make_async_remote_copy(
            src_ref=own_ref.at[h],
            dst_ref=halo.at[h],
            send_sem=halo_send.at[h],
            recv_sem=halo_recv.at[h],
            device_id={"seq": peer(1)},
        )

    def back_copy(h, t):
        return pltpu.make_async_remote_copy(
            src_ref=leave.at[h, t],
            dst_ref=back.at[h, t],
            send_sem=back_send.at[h, t],
            recv_sem=back_recv.at[h, t],
            device_id={"seq": peer(n - 1)},
        )

    def over(lo, hi, what):
        def step(i, c):
            what(i)
            return c

        lax.fori_loop(lo, hi, step, 0)

    def send_head(h):
        halo_copy(h).start()
        near_copy(h).start()
        over(1, n, lambda r: far_copy(h, r).start())

    def wait_head(h):
        halo_copy(h).wait_recv()
        near_copy(h).wait()
        over(1, n, lambda r: far_copy(h, r).wait_recv())

    def finish(h):
        odd = lax.rem(h, 2)

        def piece(t):
            back_copy(h, t).wait_recv()
            rows = pl.ds(pl.multiple_of(t * TILE, TILE), TILE)
            kept = pl.ds(pl.multiple_of(WINDOW + t * TILE, TILE), TILE)
            dkv_ref[h, 0, rows, :] = (
                scale * ka[odd, kept, :] + back[h, t, 0].astype(F32)
            ).astype(BF16)
            dkv_ref[h, 1, rows, :] = (va[odd, kept, :] + back[h, t, 1].astype(F32)).astype(BF16)

        over(0, tiles, piece)

    send_head(0)
    send_head(1)

    def head(h):
        wait_head(h)

        @pl.when(h + 2 < heads)
        def _():
            send_head(h + 2)

        odd = lax.rem(h, 2)

        def move(i):
            for s in range(LIVE):
                cur[i * LIVE + s] = recv[h, i, s]

        over(0, n, move)
        kx[:WINDOW, :] = halo[h, 0]
        kx[WINDOW:, :] = own_ref[h, 0]
        vx[:WINDOW, :] = halo[h, 1]
        vx[WINDOW:, :] = own_ref[h, 1]
        ka[odd] = jnp.zeros_like(ka[odd])
        va[odd] = jnp.zeros_like(va[odd])

        def tile(t):
            refs = (
                slot_ref, count_ref, q_ref, g_ref, o_ref, dq_ref, cur,
                kx, vx, km, vm, s_ref, dp_ref, p_ref, ds_ref,
            )
            attend_tile(refs, t, me, h, ka.at[odd], va.at[odd])
            rows = pl.ds(pl.multiple_of(t * TILE, TILE), TILE)
            leave[h, t, 0] = (scale * ka[odd, rows, :]).astype(BF16)
            leave[h, t, 1] = va[odd, rows, :].astype(BF16)
            back_copy(h, t).start()

        over(0, tiles, tile)

        @pl.when(h > 0)
        def _():
            finish(h - 1)

    over(0, heads, head)
    finish(heads - 1)

    def drain(h):
        halo_copy(h).wait_send()
        over(1, n, lambda r: far_copy(h, r).wait_send())
        over(0, tiles, lambda t: back_copy(h, t).wait_send())

    over(0, heads, drain)


def exchange(slots, counts, q, g, own, sent, n):
    heads, tokens = q.shape[:2]
    tiles = tokens // TILE
    span = WINDOW + TILE
    total = span + TOPK * BLOCK
    halves = TILE // BLOCK
    pairs = heads * tiles * total * TILE
    vmem = pl.BlockSpec(memory_space=pltpu.VMEM)
    smem = pl.BlockSpec(memory_space=pltpu.SMEM)
    hbm = pl.BlockSpec(memory_space=pl.ANY)
    dma = pltpu.SemaphoreType.DMA
    return pl.pallas_call(
        functools.partial(exchange_body, heads, n),
        in_specs=[smem, smem, vmem, vmem, vmem, hbm],
        out_specs=[vmem, vmem, vmem],
        out_shape=[
            jax.ShapeDtypeStruct(q.shape, BF16),
            jax.ShapeDtypeStruct(q.shape, BF16),
            jax.ShapeDtypeStruct((heads, 2, tokens, 128), BF16),
        ],
        scratch_shapes=[
            pltpu.VMEM((heads, n, LIVE, 2, BLOCK, 128), BF16),
            pltpu.VMEM((heads, 2, WINDOW, 128), BF16),
            pltpu.VMEM((heads, tiles, 2, TILE, 128), BF16),
            pltpu.VMEM((heads, tiles, 2, TILE, 128), BF16),
            pltpu.VMEM((n * LIVE, 2, BLOCK, 128), BF16),
            pltpu.VMEM((2 * WINDOW, 128), BF16),
            pltpu.VMEM((2 * WINDOW, 128), BF16),
            pltpu.VMEM((halves, TOPK * BLOCK, 128), BF16),
            pltpu.VMEM((halves, TOPK * BLOCK, 128), BF16),
            pltpu.VMEM((total, TILE), F32),
            pltpu.VMEM((total, TILE), F32),
            pltpu.VMEM((total, TILE), BF16),
            pltpu.VMEM((total, TILE), BF16),
            pltpu.VMEM((2, 2 * WINDOW, 128), F32),
            pltpu.VMEM((2, 2 * WINDOW, 128), F32),
            dma((heads, n)), dma((heads, n)), dma((heads,)),
            dma((heads,)), dma((heads,)), dma((heads, tiles)), dma((heads, tiles)),
        ],
        compiler_params=pltpu.CompilerParams(
            vmem_limit_bytes=VMEM, collective_id=0, has_side_effects=True
        ),
        cost_estimate=pl.CostEstimate(
            flops=pairs * 128 * 12, bytes_accessed=heads * 6 * 2**20, transcendentals=pairs
        ),
        name="exchange_attend",
    )(slots, counts, q, g, own, sent)


def share_body(n, m, row_ref, all_ref, near, mine, near_send, near_recv, far_send, far_recv):
    me = lax.axis_index("seq")
    hd = lax.axis_index("head")
    barrier = pltpu.get_barrier_semaphore()

    def over(lo, hi, what):
        def step(i, c):
            what(i)
            return c

        lax.fori_loop(lo, hi, step, 0)

    def far_peer(r):
        return {"seq": lax.rem(me + r, n)}

    def near_peer(r):
        return {"head": lax.rem(hd + r, m)}

    over(1, n, lambda r: pl.semaphore_signal(barrier, inc=1, device_id=far_peer(r)))
    over(1, m, lambda r: pl.semaphore_signal(barrier, inc=1, device_id=near_peer(r)))
    pl.semaphore_wait(barrier, n + m - 2)

    def near_copy(r):
        return pltpu.make_async_remote_copy(
            src_ref=row_ref,
            dst_ref=near.at[hd],
            send_sem=near_send.at[r],
            recv_sem=near_recv.at[r],
            device_id=near_peer(r),
        )

    def far_copy(r):
        return pltpu.make_async_remote_copy(
            src_ref=mine,
            dst_ref=all_ref.at[me],
            send_sem=far_send.at[r],
            recv_sem=far_recv.at[r],
            device_id=far_peer(r),
        )

    over(1, m, lambda r: near_copy(r).start())
    near[hd] = row_ref[...]
    over(1, m, lambda r: near_copy(r).wait_recv())
    for i in range(m):
        mine[i : i + 1, :] = near[i, 0:1, :]
    over(1, n, lambda r: far_copy(r).start())
    all_ref[me] = mine[...]
    over(1, n, lambda r: far_copy(r).wait_recv())
    over(1, m, lambda r: near_copy(r).wait_send())
    over(1, n, lambda r: far_copy(r).wait_send())


def share_rows(row, n, m):
    dma = pltpu.SemaphoreType.DMA
    vmem = pl.BlockSpec(memory_space=pltpu.VMEM)
    return pl.pallas_call(
        functools.partial(share_body, n, m),
        in_specs=[vmem],
        out_specs=vmem,
        out_shape=jax.ShapeDtypeStruct((n, m, 128), jnp.int32),
        scratch_shapes=[
            pltpu.VMEM((m, 8, 128), jnp.int32),
            pltpu.VMEM((m, 128), jnp.int32),
            dma((m,)), dma((m,)), dma((n,)), dma((n,)),
        ],
        compiler_params=pltpu.CompilerParams(collective_id=1, has_side_effects=True),
        name="share_rows",
    )(row)


def join_body(heads, o_ref, dq_ref, dkv_ref, o_out, dq_out, dk_out, dv_out):
    perm = heads_to_rows(256, heads)
    per = 256 // heads
    for part in range(o_out.shape[0] // 256):
        src = slice(part * per, (part + 1) * per)
        dst = slice(part * 256, (part + 1) * 256)
        o = jnp.concatenate([o_ref[h, src, :] for h in range(heads)], 0)
        dq = jnp.concatenate([dq_ref[h, src, :] for h in range(heads)], 0)
        both = dot(perm, jnp.concatenate([o, dq], 1)).astype(BF16)
        o_out[dst, :] = both[:, :128]
        dq_out[dst, :] = both[:, 128:]
        dk = jnp.concatenate([dkv_ref[h, 0, src, :] for h in range(heads)], 0)
        dv = jnp.concatenate([dkv_ref[h, 1, src, :] for h in range(heads)], 0)
        both = dot(perm, jnp.concatenate([dk, dv], 1)).astype(BF16)
        dk_out[dst, :] = both[:, :128]
        dv_out[dst, :] = both[:, 128:]


def join_heads(o, dq, dkv):
    heads, tokens = o.shape[:2]
    steps = 4
    hm = pl.BlockSpec((heads, tokens // steps, 128), lambda i: (0, i, 0))
    kv = pl.BlockSpec((heads, 2, tokens // steps, 128), lambda i: (0, 0, i, 0))
    out = pl.BlockSpec((tokens * heads // steps, 128), lambda i: (i, 0))
    return pl.pallas_call(
        functools.partial(join_body, heads),
        grid=(steps,),
        in_specs=[hm, hm, kv],
        out_specs=[out] * 4,
        out_shape=[jax.ShapeDtypeStruct((tokens * heads, 128), BF16)] * 4,
        compiler_params=pltpu.CompilerParams(vmem_limit_bytes=VMEM),
        cost_estimate=pl.CostEstimate(
            flops=4 * 2 * tokens * heads * 256 * 128,
            bytes_accessed=16 * tokens * heads * 128,
            transcendentals=0,
        ),
        name="join_heads",
    )(o, dq, dkv)


def tables(mem_blocks, mem_count, mem_local, owners):
    packed = jnp.concatenate([mem_blocks, mem_count[:, None]], 1)
    packed = jnp.broadcast_to(jnp.pad(packed, ((0, 0), (0, 128 - packed.shape[1]))), (8, 128))
    every = share_rows(packed, owners, lax.axis_size("head")).reshape(-1, 128)
    me = lax.axis_index("seq")
    rows = every.shape[0] // owners
    entries = rows * TOPK
    ids = every[:, :TOPK].reshape(owners, entries)
    count = every[:, TOPK].reshape(owners, rows)
    used = (
        jnp.arange(TOPK, dtype=jnp.int32)[None, None, :] < count[:, :, None]
    ).reshape(owners, entries)
    owner = ids // mem_local
    inside = ids % mem_local
    earlier = (
        jnp.arange(entries, dtype=jnp.int32)[None, :] < jnp.arange(entries, dtype=jnp.int32)[:, None]
    )
    same = (owner[:, :, None] == owner[:, None, :]) & used[:, None, :] & earlier[None]
    order = jnp.sum(same.astype(jnp.int32), 2)
    wanted = (
        (used & (owner == me))[:, :, None]
        & (order[:, :, None] == jnp.arange(LIVE, dtype=jnp.int32)[None, None, :])
    )
    send = jnp.sum(jnp.where(wanted, inside[:, :, None], 0), 1).reshape(owners * LIVE)
    slot = jnp.where(used, owner * LIVE + order, 0)
    pick = jnp.arange(owners, dtype=jnp.int32) == me
    mine = jnp.sum(jnp.where(pick[:, None], slot, 0), 0).reshape(rows, TOPK)
    my_count = jnp.sum(jnp.where(pick[:, None], count, 0), 0)
    live = jnp.arange(TOPK, dtype=jnp.int32)[None, :] < my_count[:, None]
    mine = jnp.where(live, mine, mine[:, :1]).reshape(entries)
    return send, mine, my_count


def shards(queries, seg_keys, seg_values, mem_keys, mem_values, mem_blocks, mem_count, grad_out):
    tokens, heads, dim = queries.shape
    owners = lax.axis_size("seq")
    mem_local = mem_keys.shape[0] // BLOCK

    def as_rows(x):
        return x.reshape(x.shape[0] * heads, dim)

    send, slots, counts = tables(mem_blocks, mem_count, mem_local, owners)
    q, g, own = split_heads(
        as_rows(queries), as_rows(grad_out), as_rows(seg_keys), as_rows(seg_values), heads
    )
    sent = pick_blocks(
        send,
        mem_keys.reshape(mem_local, BLOCK * heads, dim),
        mem_values.reshape(mem_local, BLOCK * heads, dim),
        heads,
    )
    sent = sent.reshape(heads, owners, LIVE, 2, BLOCK, dim)
    outs = join_heads(*exchange(slots, counts, q, g, own, sent, owners))
    return tuple(x.reshape(tokens, heads, dim) for x in outs)


def solution(mesh):
    wide = P("seq", "head", None)
    return jax.shard_map(
        shards,
        mesh=mesh,
        in_specs=(wide, wide, wide, wide, wide, P(("seq", "head"), None), P(("seq", "head")), wide),
        out_specs=(wide, wide, wide, wide),
        check_vma=False,
    )
```

```python
import functools
import math

import jax
import jax.numpy as jnp
from jax import lax
from jax.experimental import pallas as pl
from jax.experimental.pallas import tpu as pltpu
from jax.sharding import PartitionSpec as P

WINDOW = 1024
BLOCK = 128
TOPK = 4
LIVE = 2
MEM_DEV = 32
QB_DEV = 8
SIDE = 4
ORDER = (
    (2, 2), (1, 2), (2, 1), (3, 2), (2, 3), (0, 2), (2, 0),
    (1, 1), (3, 3), (1, 3), (3, 1), (0, 1), (0, 3), (1, 0), (3, 0),
)
TILE = 256
VMEM = 60 * 1024 * 1024
NEG = -1e30
F32 = jnp.float32
BF16 = jnp.bfloat16
NT = (((1,), (1,)), ((), ()))
TN = (((0,), (0,)), ((), ()))


def rows_to_heads(rows, heads):
    out = lax.broadcasted_iota(jnp.int32, (rows, rows), 0)
    src = lax.broadcasted_iota(jnp.int32, (rows, rows), 1)
    per = rows // heads
    return (src == heads * (out % per) + out // per).astype(BF16)


def heads_to_rows(rows, heads):
    out = lax.broadcasted_iota(jnp.int32, (rows, rows), 0)
    src = lax.broadcasted_iota(jnp.int32, (rows, rows), 1)
    per = rows // heads
    return (src == per * (out % heads) + out // heads).astype(BF16)


def dot(a, b, dims=None):
    if dims is None:
        return jnp.dot(a, b, preferred_element_type=F32)
    return lax.dot_general(a, b, dims, preferred_element_type=F32)


def attend_tile(refs, t, rank, h, ka, va):
    (plan_s, q_ref, g_ref, o_ref, dq_ref, cur, kx, vx, km, vm, s_ref, dp_ref, p_ref, ds_ref) = refs
    span = WINDOW + TILE
    total = span + TOPK * BLOCK
    halves = TILE // BLOCK
    scale = 1.0 / math.sqrt(128.0)
    to_two = scale * math.log2(math.e)
    start = pl.multiple_of(t * TILE, TILE)
    win = pl.ds(start, span)
    q = q_ref[h, pl.ds(start, TILE), :]
    g = g_ref[h, pl.ds(start, TILE), :]

    for half in range(halves):
        for e in range(TOPK):
            slot = plan_s[LIVE, rank, (t * halves + half) * TOPK + e]
            first = plan_s[LIVE, rank, (t * halves + half) * TOPK]
            slot = jnp.maximum(jnp.where(slot < 0, first, slot), 0)
            km[half, e * BLOCK : (e + 1) * BLOCK, :] = cur[slot, 0]
            vm[half, e * BLOCK : (e + 1) * BLOCK, :] = cur[slot, 1]

    s_ref[:span, :] = dot(kx[win, :], q, NT)
    dp_ref[:span, :] = dot(vx[win, :], g, NT)
    for half in range(halves):
        cols = slice(half * BLOCK, (half + 1) * BLOCK)
        far = dot(km[half], q[cols], NT)
        for e in range(TOPK):
            rows = slice(e * BLOCK, (e + 1) * BLOCK)
            s_ref[span + e * BLOCK : span + (e + 1) * BLOCK, cols] = jnp.where(
                plan_s[LIVE, rank, (t * halves + half) * TOPK + e] >= 0, far[rows], NEG
            )
        dp_ref[span:, cols] = dot(vm[half], g[cols], NT)

    row = lax.broadcasted_iota(jnp.int32, (TILE, TILE), 0)
    col = lax.broadcasted_iota(jnp.int32, (TILE, TILE), 1)
    s_ref[:TILE, :] = jnp.where(row > col, s_ref[:TILE, :], NEG)
    s_ref[WINDOW:span, :] = jnp.where(row <= col, s_ref[WINDOW:span, :], NEG)

    @pl.when(rank == 0)
    def _():
        for c in range(WINDOW // TILE):
            @pl.when(c + t < WINDOW // TILE)
            def _():
                s_ref[c * TILE : (c + 1) * TILE, :] = jnp.full((TILE, TILE), NEG, F32)

    steps = total // BLOCK

    def chunk(c):
        return pl.ds(pl.multiple_of(c * BLOCK, BLOCK), BLOCK)

    def fold(x, op):
        return op(x.reshape(BLOCK // 8, 8, TILE), 0)

    def top_step(c, top):
        return jnp.maximum(top, fold(s_ref[chunk(c), :], jnp.max))

    top = lax.fori_loop(0, steps, top_step, jnp.full((8, TILE), NEG, F32), unroll=2)
    top = jnp.max(top, 0, keepdims=True) * to_two

    def exp_step(c, acc):
        e = jnp.exp2(s_ref[chunk(c), :] * to_two - top)
        s_ref[chunk(c), :] = e
        return acc + fold(e, jnp.sum)

    acc = lax.fori_loop(0, steps, exp_step, jnp.zeros((8, TILE), F32), unroll=2)
    inv = 1.0 / jnp.sum(acc, 0, keepdims=True)

    def prob_step(c, acc):
        p = s_ref[chunk(c), :] * inv
        s_ref[chunk(c), :] = p
        p_ref[chunk(c), :] = p.astype(BF16)
        return acc + fold(p * dp_ref[chunk(c), :], jnp.sum)

    acc = lax.fori_loop(0, steps, prob_step, jnp.zeros((8, TILE), F32), unroll=2)
    delta = jnp.sum(acc, 0, keepdims=True)

    def score_step(c, carry):
        ds_ref[chunk(c), :] = (s_ref[chunk(c), :] * (dp_ref[chunk(c), :] - delta)).astype(BF16)
        return carry

    lax.fori_loop(0, steps, score_step, 0, unroll=2)

    o = dot(p_ref[:span, :], vx[win, :], TN)
    dq = dot(ds_ref[:span, :], kx[win, :], TN)
    for half in range(halves):
        cols = slice(half * BLOCK, (half + 1) * BLOCK)
        dst = pl.ds(pl.multiple_of(start + half * BLOCK, BLOCK), BLOCK)
        o_ref[h, dst, :] = (o[cols] + dot(p_ref[span:, cols], vm[half], TN)).astype(BF16)
        dq_ref[h, dst, :] = (
            scale * (dq[cols] + dot(ds_ref[span:, cols], km[half], TN))
        ).astype(BF16)
    va[win, :] += dot(p_ref[:span, :], g)
    ka[win, :] += dot(ds_ref[:span, :], q)


def exchange_body(
    heads, n, m, ids_ref, used_ref, q_hbm, g_hbm, k_hbm, v_hbm, mk_hbm, mv_hbm,
    o_ref, dq_ref, dkv_ref,
    raw, mem, q_ref, g_ref, own_ref, sent_ref, near_tab, my_tab, far_tab, flat, plan, plan_s,
    recv, halo, leave, back, cur, kx, vx, km, vm, s_ref, dp_ref, p_ref, ds_ref, ka, va,
    load_sem, plan_sem, tab_near_send, tab_near_recv, tab_far_send, tab_far_recv,
    far_send, far_recv, near, halo_send, halo_recv, back_send, back_recv,
):
    me = lax.axis_index("seq")
    hd = lax.axis_index("head")
    tiles = WINDOW // TILE
    scale = 1.0 / math.sqrt(128.0)
    barrier = pltpu.get_barrier_semaphore()

    def over(lo, hi, what, unroll=None):
        def step(i, c):
            what(i)
            return c

        lax.fori_loop(lo, hi, step, 0, unroll=unroll)

    def peer(r):
        return lax.rem(me + r, n)

    def shifted(k):
        dz, dx = ORDER[k]
        return lax.rem(me // SIDE + dz, SIDE) * SIDE + lax.rem(lax.rem(me, SIDE) + dx, SIDE)

    def head_peer(r):
        return {"head": lax.rem(hd + r, m)}

    loads = [
        pltpu.make_async_copy(src, raw.at[i], load_sem.at[i])
        for i, src in enumerate((k_hbm, v_hbm, q_hbm, g_hbm))
    ] + [
        pltpu.make_async_copy(src, mem.at[i], load_sem.at[4 + i])
        for i, src in enumerate((mk_hbm, mv_hbm))
    ]
    for load in loads:
        load.start()

    over(1, n, lambda r: pl.semaphore_signal(barrier, inc=1, device_id={"seq": peer(r)}))
    over(1, m, lambda r: pl.semaphore_signal(barrier, inc=1, device_id=head_peer(r)))

    lane = lax.broadcasted_iota(jnp.int32, (8, 128), 1)
    row = jnp.zeros((8, 128), jnp.int32)
    for e in range(TOPK):
        value = jnp.where(e < used_ref[0], ids_ref[0, e] + 1, 0)
        row = jnp.where(lane == hd * TOPK + e, value, row)
    near_tab[hd] = row
    pl.semaphore_wait(barrier, n + m - 2)

    def tab_near(r):
        return pltpu.make_async_remote_copy(
            src_ref=near_tab.at[hd],
            dst_ref=near_tab.at[hd],
            send_sem=tab_near_send.at[r],
            recv_sem=tab_near_recv.at[r],
            device_id=head_peer(r),
        )

    def tab_far(r):
        return pltpu.make_async_remote_copy(
            src_ref=my_tab,
            dst_ref=far_tab.at[me],
            send_sem=tab_far_send.at[r],
            recv_sem=tab_far_recv.at[r],
            device_id={"seq": peer(r)},
        )

    def far_copy(h, k):
        return pltpu.make_async_remote_copy(
            src_ref=sent_ref.at[h, shifted(k)],
            dst_ref=recv.at[h, me],
            send_sem=far_send.at[h, k],
            recv_sem=far_recv.at[h, k],
            device_id={"seq": shifted(k)},
        )

    def near_copy(h):
        return pltpu.make_async_copy(sent_ref.at[h, me], recv.at[h, me], near.at[h])

    def halo_copy(h):
        return pltpu.make_async_remote_copy(
            src_ref=own_ref.at[h],
            dst_ref=halo.at[h],
            send_sem=halo_send.at[h],
            recv_sem=halo_recv.at[h],
            device_id={"seq": peer(1)},
        )

    def back_copy(h, t):
        return pltpu.make_async_remote_copy(
            src_ref=leave.at[h, t],
            dst_ref=back.at[h, t],
            send_sem=back_send.at[h, t],
            recv_sem=back_recv.at[h, t],
            device_id={"seq": peer(n - 1)},
        )

    over(1, m, lambda r: tab_near(r).start())

    perm = rows_to_heads(256, heads)
    per = 256 // heads

    def split(left, right, left_out, right_out):
        both = dot(perm, jnp.concatenate([left, right], 1)).astype(BF16)
        for h in range(heads):
            left_out(h, both[h * per : (h + 1) * per, :128])
            right_out(h, both[h * per : (h + 1) * per, 128:])

    def put(ref, *at):
        def store(h, x):
            ref[(h, *at)] = x

        return store

    def spans(i):
        return (
            pl.ds(pl.multiple_of(i * 256, 256), 256),
            pl.ds(pl.multiple_of(i * per, per), per),
        )

    def split_kv(i):
        src, dst = spans(i)
        split(raw[0, src, :], raw[1, src, :], put(own_ref, 0, dst), put(own_ref, 1, dst))

    def split_qg(i):
        src, dst = spans(i)
        split(raw[2, src, :], raw[3, src, :], put(q_ref, dst), put(g_ref, dst))

    parts = WINDOW * heads // 256
    loads[0].wait()
    loads[1].wait()
    over(0, parts, split_kv, unroll=2)
    halo_copy(0).start()
    halo_copy(1).start()

    over(1, m, lambda r: tab_near(r).wait_recv())
    total = near_tab[0]
    for i in range(1, m):
        total = total + near_tab[i]
    my_tab[...] = total
    far_tab[me] = total
    over(1, n, lambda r: tab_far(r).start())

    loads[2].wait()
    loads[3].wait()
    over(0, parts, split_qg, unroll=2)
    over(1, n, lambda r: tab_far(r).wait_recv())

    for d in range(n):
        flat[d : d + 1, :] = far_tab[d, 0:1, :]
    table = flat[...] - 1
    owner = lax.shift_right_arithmetic(table, 5)
    inside = lax.bitwise_and(table, MEM_DEV - 1)
    live = table >= 0
    order = jnp.zeros_like(table)
    for shift in range(1, QB_DEV * TOPK):
        same = (pltpu.roll(owner, shift, 1) == owner) & live
        order = order + same.astype(jnp.int32)
    for k in range(LIVE):
        x = jnp.where(live & (owner == me) & (order == k), inside, 0)
        for shift in (1, 2, 4, 8, 16):
            x = x + pltpu.roll(x, shift, 1)
        plan[k] = x
    plan[LIVE] = jnp.where(live, owner * LIVE + order, -1)
    to_scalar = pltpu.make_async_copy(plan, plan_s, plan_sem)
    to_scalar.start()
    loads[4].wait()
    loads[5].wait()
    to_scalar.wait()
    last = QB_DEV * TOPK - 1

    def pick(d):
        for k in range(LIVE):
            block = plan_s[k, d, last]
            for part in range(BLOCK * heads // 256):
                src = slice(part * 256, (part + 1) * 256)
                dst = slice(part * per, (part + 1) * per)
                split(
                    mem[0, block, src, :],
                    mem[1, block, src, :],
                    put(sent_ref, d, k, 0, dst),
                    put(sent_ref, d, k, 1, dst),
                )

    for k in range(n - 1):
        pick(shifted(k))
        far_copy(0, k).start()
    pick(me)
    near_copy(0).start()

    def send_far(h):
        near_copy(h).start()
        for k in range(n - 1):
            far_copy(h, k).start()

    send_far(1)

    def wait_head(h):
        halo_copy(h).wait_recv()
        near_copy(h).wait()
        for k in range(n - 1):
            far_copy(h, k).wait_recv()

    def finish(h):
        odd = lax.rem(h, 2)

        def piece(t):
            back_copy(h, t).wait_recv()
            rows = pl.ds(pl.multiple_of(t * TILE, TILE), TILE)
            kept = pl.ds(pl.multiple_of(WINDOW + t * TILE, TILE), TILE)
            dkv_ref[h, 0, rows, :] = (
                scale * ka[odd, kept, :] + back[h, t, 0].astype(F32)
            ).astype(BF16)
            dkv_ref[h, 1, rows, :] = (va[odd, kept, :] + back[h, t, 1].astype(F32)).astype(BF16)

        over(0, tiles, piece)

    def head(h):
        wait_head(h)

        @pl.when(h + 2 < heads)
        def _():
            halo_copy(h + 2).start()
            send_far(h + 2)

        odd = lax.rem(h, 2)

        def move(i):
            for s in range(LIVE):
                cur[i * LIVE + s] = recv[h, i, s]

        over(0, n, move)
        kx[:WINDOW, :] = halo[h, 0]
        kx[WINDOW:, :] = own_ref[h, 0]
        vx[:WINDOW, :] = halo[h, 1]
        vx[WINDOW:, :] = own_ref[h, 1]
        ka[odd] = jnp.zeros_like(ka[odd])
        va[odd] = jnp.zeros_like(va[odd])

        def tile(t):
            refs = (
                plan_s, q_ref, g_ref, o_ref, dq_ref, cur,
                kx, vx, km, vm, s_ref, dp_ref, p_ref, ds_ref,
            )
            attend_tile(refs, t, me, h, ka.at[odd], va.at[odd])
            rows = pl.ds(pl.multiple_of(t * TILE, TILE), TILE)
            leave[h, t, 0] = (scale * ka[odd, rows, :]).astype(BF16)
            leave[h, t, 1] = va[odd, rows, :].astype(BF16)
            back_copy(h, t).start()

        over(0, tiles, tile)

        @pl.when(h > 0)
        def _():
            finish(h - 1)

    over(0, heads, head)
    finish(heads - 1)

    over(1, m, lambda r: tab_near(r).wait_send())
    over(1, n, lambda r: tab_far(r).wait_send())

    def drain(h):
        halo_copy(h).wait_send()
        for k in range(n - 1):
            far_copy(h, k).wait_send()
        over(0, tiles, lambda t: back_copy(h, t).wait_send())

    over(0, heads, drain)


def exchange(ids, used, q, g, k, v, mem_k, mem_v, heads, n, m):
    rows = q.shape[0]
    tokens = rows // heads
    tiles = tokens // TILE
    span = WINDOW + TILE
    total = span + TOPK * BLOCK
    halves = TILE // BLOCK
    pairs = heads * tiles * total * TILE
    vmem = pl.BlockSpec(memory_space=pltpu.VMEM)
    smem = pl.BlockSpec(memory_space=pltpu.SMEM)
    hbm = pl.BlockSpec(memory_space=pl.ANY)
    dma = pltpu.SemaphoreType.DMA
    by_head = (heads, tokens, 128)
    by_pair = (heads, 2, tokens, 128)
    return pl.pallas_call(
        functools.partial(exchange_body, heads, n, m),
        in_specs=[smem, smem] + [hbm] * 6,
        out_specs=[vmem, vmem, vmem],
        out_shape=[
            jax.ShapeDtypeStruct(by_head, BF16),
            jax.ShapeDtypeStruct(by_head, BF16),
            jax.ShapeDtypeStruct(by_pair, BF16),
        ],
        scratch_shapes=[
            pltpu.VMEM((4, rows, 128), BF16),
            pltpu.VMEM((2,) + mem_k.shape, BF16),
            pltpu.VMEM(by_head, BF16),
            pltpu.VMEM(by_head, BF16),
            pltpu.VMEM(by_pair, BF16),
            pltpu.VMEM((heads, n, LIVE, 2, BLOCK, 128), BF16),
            pltpu.VMEM((m, 8, 128), jnp.int32),
            pltpu.VMEM((8, 128), jnp.int32),
            pltpu.VMEM((n, 8, 128), jnp.int32),
            pltpu.VMEM((n, 128), jnp.int32),
            pltpu.VMEM((LIVE + 1, n, 128), jnp.int32),
            pltpu.SMEM((LIVE + 1, n, 128), jnp.int32),
            pltpu.VMEM((heads, n, LIVE, 2, BLOCK, 128), BF16),
            pltpu.VMEM((heads, 2, WINDOW, 128), BF16),
            pltpu.VMEM((heads, tiles, 2, TILE, 128), BF16),
            pltpu.VMEM((heads, tiles, 2, TILE, 128), BF16),
            pltpu.VMEM((n * LIVE, 2, BLOCK, 128), BF16),
            pltpu.VMEM((2 * WINDOW, 128), BF16),
            pltpu.VMEM((2 * WINDOW, 128), BF16),
            pltpu.VMEM((halves, TOPK * BLOCK, 128), BF16),
            pltpu.VMEM((halves, TOPK * BLOCK, 128), BF16),
            pltpu.VMEM((total, TILE), F32),
            pltpu.VMEM((total, TILE), F32),
            pltpu.VMEM((total, TILE), BF16),
            pltpu.VMEM((total, TILE), BF16),
            pltpu.VMEM((2, 2 * WINDOW, 128), F32),
            pltpu.VMEM((2, 2 * WINDOW, 128), F32),
            dma((6,)), dma, dma((m,)), dma((m,)), dma((n,)), dma((n,)),
            dma((heads, n)), dma((heads, n)), dma((heads,)),
            dma((heads,)), dma((heads,)), dma((heads, tiles)), dma((heads, tiles)),
        ],
        compiler_params=pltpu.CompilerParams(
            vmem_limit_bytes=VMEM, collective_id=0, has_side_effects=True
        ),
        cost_estimate=pl.CostEstimate(
            flops=pairs * 128 * 12, bytes_accessed=heads * 6 * 2**20, transcendentals=pairs
        ),
        name="exchange_attend",
    )(ids, used, q, g, k, v, mem_k, mem_v)


def join_body(heads, o_ref, dq_ref, dkv_ref, o_out, dq_out, dk_out, dv_out):
    perm = heads_to_rows(256, heads)
    per = 256 // heads
    for part in range(o_out.shape[0] // 256):
        src = slice(part * per, (part + 1) * per)
        dst = slice(part * 256, (part + 1) * 256)
        o = jnp.concatenate([o_ref[h, src, :] for h in range(heads)], 0)
        dq = jnp.concatenate([dq_ref[h, src, :] for h in range(heads)], 0)
        both = dot(perm, jnp.concatenate([o, dq], 1)).astype(BF16)
        o_out[dst, :] = both[:, :128]
        dq_out[dst, :] = both[:, 128:]
        dk = jnp.concatenate([dkv_ref[h, 0, src, :] for h in range(heads)], 0)
        dv = jnp.concatenate([dkv_ref[h, 1, src, :] for h in range(heads)], 0)
        both = dot(perm, jnp.concatenate([dk, dv], 1)).astype(BF16)
        dk_out[dst, :] = both[:, :128]
        dv_out[dst, :] = both[:, 128:]


def join_heads(o, dq, dkv):
    heads, tokens = o.shape[:2]
    steps = 4
    hm = pl.BlockSpec((heads, tokens // steps, 128), lambda i: (0, i, 0))
    kv = pl.BlockSpec((heads, 2, tokens // steps, 128), lambda i: (0, 0, i, 0))
    out = pl.BlockSpec((tokens * heads // steps, 128), lambda i: (i, 0))
    return pl.pallas_call(
        functools.partial(join_body, heads),
        grid=(steps,),
        in_specs=[hm, hm, kv],
        out_specs=[out] * 4,
        out_shape=[jax.ShapeDtypeStruct((tokens * heads, 128), BF16)] * 4,
        compiler_params=pltpu.CompilerParams(vmem_limit_bytes=VMEM),
        cost_estimate=pl.CostEstimate(
            flops=4 * 2 * tokens * heads * 256 * 128,
            bytes_accessed=16 * tokens * heads * 128,
            transcendentals=0,
        ),
        name="join_heads",
    )(o, dq, dkv)


def shards(queries, seg_keys, seg_values, mem_keys, mem_values, mem_blocks, mem_count, grad_out):
    tokens, heads, dim = queries.shape
    mem_local = mem_keys.shape[0] // BLOCK

    def as_rows(x):
        return x.reshape(x.shape[0] * heads, dim)

    def as_blocks(x):
        return x.reshape(mem_local, BLOCK * heads, dim)

    outs = exchange(
        mem_blocks, mem_count,
        as_rows(queries), as_rows(grad_out), as_rows(seg_keys), as_rows(seg_values),
        as_blocks(mem_keys), as_blocks(mem_values),
        heads, lax.axis_size("seq"), lax.axis_size("head"),
    )
    return tuple(x.reshape(tokens, heads, dim) for x in join_heads(*outs))


def solution(mesh):
    wide = P("seq", "head", None)
    return jax.shard_map(
        shards,
        mesh=mesh,
        in_specs=(wide, wide, wide, wide, wide, P(("seq", "head"), None), P(("seq", "head")), wide),
        out_specs=(wide, wide, wide, wide),
        check_vma=False,
    )
```

```python
import functools
import math

import jax
import jax.numpy as jnp
from jax import lax
from jax.experimental import pallas as pl
from jax.experimental.pallas import tpu as pltpu
from jax.sharding import PartitionSpec as P

WINDOW = 1024
BLOCK = 128
TOPK = 4
LIVE = 2
MEM_DEV = 32
QB_DEV = 8
SIDE = 4
ORDER = (
    (2, 2), (1, 2), (2, 1), (3, 2), (2, 3), (0, 2), (2, 0),
    (1, 1), (3, 3), (1, 3), (3, 1), (0, 1), (0, 3), (1, 0), (3, 0),
)
TILE = 256
HALF = 512
VMEM = 60 * 1024 * 1024
NEG = -1e30
F32 = jnp.float32
BF16 = jnp.bfloat16
NT = (((1,), (1,)), ((), ()))
TN = (((0,), (0,)), ((), ()))


def rows_to_heads(rows, heads):
    out = lax.broadcasted_iota(jnp.int32, (rows, rows), 0)
    src = lax.broadcasted_iota(jnp.int32, (rows, rows), 1)
    per = rows // heads
    return (src == heads * (out % per) + out // per).astype(BF16)


def heads_to_rows(rows, heads):
    out = lax.broadcasted_iota(jnp.int32, (rows, rows), 0)
    src = lax.broadcasted_iota(jnp.int32, (rows, rows), 1)
    per = rows // heads
    return (src == per * (out % heads) + out // heads).astype(BF16)


def dot(a, b, dims=None):
    if dims is None:
        return jnp.dot(a, b, preferred_element_type=F32)
    return lax.dot_general(a, b, dims, preferred_element_type=F32)


def attend_tile(refs, t, rank, h, ka, va):
    (plan_s, qg_ref, o_ref, dq_ref, stat, cur, kx, vx, km, vm, s_ref, dp_ref, p_ref, ds_ref) = refs
    span = WINDOW + TILE
    total = span + TOPK * BLOCK
    halves = TILE // BLOCK
    scale = 1.0 / math.sqrt(128.0)
    to_two = scale * math.log2(math.e)
    start = pl.multiple_of(t * TILE, TILE)
    win = pl.ds(start, span)
    q = qg_ref[h, 0, pl.ds(start, TILE), :]
    g = qg_ref[h, 1, pl.ds(start, TILE), :]

    for half in range(halves):
        for e in range(TOPK):
            slot = plan_s[LIVE, rank, (t * halves + half) * TOPK + e]
            first = plan_s[LIVE, rank, (t * halves + half) * TOPK]
            slot = jnp.maximum(jnp.where(slot < 0, first, slot), 0)
            km[half, e * BLOCK : (e + 1) * BLOCK, :] = cur[slot, 0]
            vm[half, e * BLOCK : (e + 1) * BLOCK, :] = cur[slot, 1]

    s_ref[:span, :] = dot(kx[win, :], q, NT)
    dp_ref[:span, :] = dot(vx[win, :], g, NT)
    for half in range(halves):
        cols = slice(half * BLOCK, (half + 1) * BLOCK)
        far = dot(km[half], q[cols], NT)
        for e in range(TOPK):
            rows = slice(e * BLOCK, (e + 1) * BLOCK)
            s_ref[span + e * BLOCK : span + (e + 1) * BLOCK, cols] = jnp.where(
                plan_s[LIVE, rank, (t * halves + half) * TOPK + e] >= 0, far[rows], NEG
            )
        dp_ref[span:, cols] = dot(vm[half], g[cols], NT)

    row = lax.broadcasted_iota(jnp.int32, (TILE, TILE), 0)
    col = lax.broadcasted_iota(jnp.int32, (TILE, TILE), 1)
    s_ref[:TILE, :] = jnp.where(row > col, s_ref[:TILE, :], NEG)
    s_ref[WINDOW:span, :] = jnp.where(row <= col, s_ref[WINDOW:span, :], NEG)

    @pl.when(rank == 0)
    def _():
        for c in range(WINDOW // TILE):
            @pl.when(c + t < WINDOW // TILE)
            def _():
                s_ref[c * TILE : (c + 1) * TILE, :] = jnp.full((TILE, TILE), NEG, F32)

    steps = total // BLOCK

    def chunk(c):
        return pl.ds(pl.multiple_of(c * BLOCK, BLOCK), BLOCK)

    def fold(x, op):
        return op(x.reshape(BLOCK // 8, 8, TILE), 0)

    def top_step(c, top):
        return jnp.maximum(top, fold(s_ref[chunk(c), :], jnp.max))

    top = lax.fori_loop(0, steps, top_step, jnp.full((8, TILE), NEG, F32), unroll=7)
    top = jnp.max(top, 0, keepdims=True) * to_two

    def exp_step(c, accs):
        e = jnp.exp2(s_ref[chunk(c), :] * to_two - top)
        s_ref[chunk(c), :] = e
        return accs[0] + fold(e, jnp.sum), accs[1] + fold(e * dp_ref[chunk(c), :], jnp.sum)

    zero = jnp.zeros((8, TILE), F32)
    mass, delta = lax.fori_loop(0, steps, exp_step, (zero, zero), unroll=7)
    mass = jnp.sum(mass, 0, keepdims=True)
    inv = 1.0 / mass
    delta = jnp.sum(delta, 0, keepdims=True) * inv
    stat[h, t, 0:1, :] = top + jnp.log(mass) * math.log2(math.e)
    stat[h, t, 1:2, :] = delta

    def prob_step(c, carry):
        p = s_ref[chunk(c), :] * inv
        p_ref[chunk(c), :] = p.astype(BF16)
        ds_ref[chunk(c), :] = (p * (dp_ref[chunk(c), :] - delta)).astype(BF16)
        return carry

    lax.fori_loop(0, steps, prob_step, 0, unroll=7)

    o = dot(p_ref[:span, :], vx[win, :], TN)
    dq = dot(ds_ref[:span, :], kx[win, :], TN)
    for half in range(halves):
        cols = slice(half * BLOCK, (half + 1) * BLOCK)
        dst = pl.ds(pl.multiple_of(start + half * BLOCK, BLOCK), BLOCK)
        o_ref[h, dst, :] = (o[cols] + dot(p_ref[span:, cols], vm[half], TN)).astype(BF16)
        dq_ref[h, dst, :] = (
            scale * (dq[cols] + dot(ds_ref[span:, cols], km[half], TN))
        ).astype(BF16)

    def own_keys(b, carry):
        src = pl.ds(pl.multiple_of(WINDOW + (b - t) * TILE, TILE), TILE)
        dst = pl.ds(pl.multiple_of(b * TILE, TILE), TILE)
        va[dst, :] += dot(p_ref[src, :], g)
        ka[dst, :] += dot(ds_ref[src, :], q)
        return carry

    lax.fori_loop(0, t + 1, own_keys, 0)


def next_tile(h, t, rank, n, own_ref, next_ref, stat_in, ka, va):
    scale = 1.0 / math.sqrt(128.0)
    to_two = scale * math.log2(math.e)
    cols = pl.ds(pl.multiple_of(t * TILE, TILE), TILE)
    q = next_ref[h, 0, cols, :]
    g = next_ref[h, 1, cols, :]
    lse = jnp.where(rank == n - 1, -NEG, stat_in[h, t, 0:1, :])
    delta = stat_in[h, t, 1:2, :]
    row = lax.broadcasted_iota(jnp.int32, (TILE, TILE), 0)
    col = lax.broadcasted_iota(jnp.int32, (TILE, TILE), 1)

    def keys(b, carry):
        rows = pl.ds(pl.multiple_of(b * TILE, TILE), TILE)
        s = dot(own_ref[h, 0, rows, :], q, NT)
        s = jnp.where(row + (b - t) * TILE > col, s * to_two, NEG)
        p = jnp.exp2(s - lse)
        ds = p * (dot(own_ref[h, 1, rows, :], g, NT) - delta)
        va[rows, :] += dot(p.astype(BF16), g)
        ka[rows, :] += dot(ds.astype(BF16), q)
        return carry

    lax.fori_loop(t, WINDOW // TILE, keys, 0)


def exchange_body(
    heads, n, m, ids_ref, used_ref, q_hbm, g_hbm, k_hbm, v_hbm, mk_hbm, mv_hbm,
    o_ref, dq_ref, dkv_ref,
    raw, mem, qg_ref, own_ref, sent_ref, near_tab, my_tab, far_tab, flat, plan, plan_s,
    recv, halo, ahead, stat, stat_in, cur, kx, vx, km, vm, s_ref, dp_ref, p_ref, ds_ref, ka, va,
    load_sem, plan_sem, tab_near_send, tab_near_recv, tab_far_send, tab_far_recv,
    far_send, far_recv, near, halo_send, halo_recv, ahead_send, ahead_recv, stat_send, stat_recv,
):
    me = lax.axis_index("seq")
    hd = lax.axis_index("head")
    tiles = WINDOW // TILE
    scale = 1.0 / math.sqrt(128.0)
    barrier = pltpu.get_barrier_semaphore()

    def over(lo, hi, what, unroll=None):
        def step(i, c):
            what(i)
            return c

        lax.fori_loop(lo, hi, step, 0, unroll=unroll)

    def peer(r):
        return lax.rem(me + r, n)

    def shifted(k):
        dz, dx = ORDER[k]
        return lax.rem(me // SIDE + dz, SIDE) * SIDE + lax.rem(lax.rem(me, SIDE) + dx, SIDE)

    def head_peer(r):
        return {"head": lax.rem(hd + r, m)}

    loads = [
        pltpu.make_async_copy(src, raw.at[i], load_sem.at[i])
        for i, src in enumerate((k_hbm, v_hbm, q_hbm, g_hbm))
    ] + [
        pltpu.make_async_copy(src, mem.at[i], load_sem.at[4 + i])
        for i, src in enumerate((mk_hbm, mv_hbm))
    ]
    for load in loads:
        load.start()

    over(1, n, lambda r: pl.semaphore_signal(barrier, inc=1, device_id={"seq": peer(r)}))
    over(1, m, lambda r: pl.semaphore_signal(barrier, inc=1, device_id=head_peer(r)))

    lane = lax.broadcasted_iota(jnp.int32, (8, 128), 1)
    row = jnp.zeros((8, 128), jnp.int32)
    for e in range(TOPK):
        value = jnp.where(e < used_ref[0], ids_ref[0, e] + 1, 0)
        row = jnp.where(lane == hd * TOPK + e, value, row)
    near_tab[hd] = row
    pl.semaphore_wait(barrier, n + m - 2)

    def tab_near(r):
        return pltpu.make_async_remote_copy(
            src_ref=near_tab.at[hd],
            dst_ref=near_tab.at[hd],
            send_sem=tab_near_send.at[r],
            recv_sem=tab_near_recv.at[r],
            device_id=head_peer(r),
        )

    def tab_far(r):
        return pltpu.make_async_remote_copy(
            src_ref=my_tab,
            dst_ref=far_tab.at[me],
            send_sem=tab_far_send.at[r],
            recv_sem=tab_far_recv.at[r],
            device_id={"seq": peer(r)},
        )

    def far_copy(h, k):
        return pltpu.make_async_remote_copy(
            src_ref=sent_ref.at[h, shifted(k)],
            dst_ref=recv.at[h, me],
            send_sem=far_send.at[h, k],
            recv_sem=far_recv.at[h, k],
            device_id={"seq": shifted(k)},
        )

    def near_copy(h):
        return pltpu.make_async_copy(sent_ref.at[h, me], recv.at[h, me], near.at[h])

    def quarter(j):
        return pl.ds((j % 2) * HALF, HALF)

    def halo_copy(h, j):
        return pltpu.make_async_remote_copy(
            src_ref=own_ref.at[h, j // 2, quarter(j)],
            dst_ref=halo.at[h, j // 2, quarter(j)],
            send_sem=halo_send.at[h, j],
            recv_sem=halo_recv.at[h, j],
            device_id={"seq": peer(1)},
        )

    def ahead_copy(h, j):
        return pltpu.make_async_remote_copy(
            src_ref=qg_ref.at[h, j // 2, quarter(j)],
            dst_ref=ahead.at[h, j // 2, quarter(j)],
            send_sem=ahead_send.at[h, j],
            recv_sem=ahead_recv.at[h, j],
            device_id={"seq": peer(n - 1)},
        )

    def stat_copy(h):
        return pltpu.make_async_remote_copy(
            src_ref=stat.at[h],
            dst_ref=stat_in.at[h],
            send_sem=stat_send.at[h],
            recv_sem=stat_recv.at[h],
            device_id={"seq": peer(n - 1)},
        )

    def each_part(what):
        for h in range(heads):
            for j in range(4):
                what(h, j)

    over(1, m, lambda r: tab_near(r).start())

    perm = rows_to_heads(256, heads)
    per = 256 // heads

    def split(left, right, left_out, right_out):
        both = dot(perm, jnp.concatenate([left, right], 1)).astype(BF16)
        for h in range(heads):
            left_out(h, both[h * per : (h + 1) * per, :128])
            right_out(h, both[h * per : (h + 1) * per, 128:])

    def put(ref, *at):
        def store(h, x):
            ref[(h, *at)] = x

        return store

    def spans(i):
        return (
            pl.ds(pl.multiple_of(i * 256, 256), 256),
            pl.ds(pl.multiple_of(i * per, per), per),
        )

    def split_kv(i):
        src, dst = spans(i)
        split(raw[0, src, :], raw[1, src, :], put(own_ref, 0, dst), put(own_ref, 1, dst))

    def split_qg(i):
        src, dst = spans(i)
        split(raw[2, src, :], raw[3, src, :], put(qg_ref, 0, dst), put(qg_ref, 1, dst))

    parts = WINDOW * heads // 256
    loads[0].wait()
    loads[1].wait()
    over(0, parts, split_kv, unroll=2)
    for j in range(4):
        halo_copy(0, j).start()

    over(1, m, lambda r: tab_near(r).wait_recv())
    total = near_tab[0]
    for i in range(1, m):
        total = total + near_tab[i]
    my_tab[...] = total
    far_tab[me] = total
    over(1, n, lambda r: tab_far(r).start())

    loads[2].wait()
    loads[3].wait()
    over(0, parts, split_qg, unroll=2)
    for j in range(4):
        ahead_copy(0, j).start()
    over(1, n, lambda r: tab_far(r).wait_recv())

    for d in range(n):
        flat[d : d + 1, :] = far_tab[d, 0:1, :]
    table = flat[...] - 1
    owner = lax.shift_right_arithmetic(table, 5)
    inside = lax.bitwise_and(table, MEM_DEV - 1)
    live = table >= 0
    order = jnp.zeros_like(table)
    for shift in range(1, QB_DEV * TOPK):
        same = (pltpu.roll(owner, shift, 1) == owner) & live
        order = order + same.astype(jnp.int32)
    for k in range(LIVE):
        x = jnp.where(live & (owner == me) & (order == k), inside, 0)
        for shift in (1, 2, 4, 8, 16):
            x = x + pltpu.roll(x, shift, 1)
        plan[k] = x
    plan[LIVE] = jnp.where(live, owner * LIVE + order, -1)
    to_scalar = pltpu.make_async_copy(plan, plan_s, plan_sem)
    to_scalar.start()
    loads[4].wait()
    loads[5].wait()
    to_scalar.wait()
    last = QB_DEV * TOPK - 1

    def pick(d):
        for k in range(LIVE):
            block = plan_s[k, d, last]
            for part in range(BLOCK * heads // 256):
                src = slice(part * 256, (part + 1) * 256)
                dst = slice(part * per, (part + 1) * per)
                split(
                    mem[0, block, src, :],
                    mem[1, block, src, :],
                    put(sent_ref, d, k, 0, dst),
                    put(sent_ref, d, k, 1, dst),
                )

    def follow(h, k):
        @pl.when(h < heads)
        def _():
            if k == 0:
                near_copy(h).start()
            if k % 4 == 0:
                halo_copy(h, k // 4).start()
                ahead_copy(h, k // 4).start()
            far_copy(h, k).start()

    for k in range(n - 1):
        pick(shifted(k))
        far_copy(0, k).start()
    pick(me)
    near_copy(0).start()

    def finish(h):
        odd = lax.rem(h, 2)
        stat_copy(h).wait_recv()
        for j in range(4):
            ahead_copy(h, j).wait_recv()
        over(
            0,
            tiles,
            lambda t: next_tile(h, t, me, n, own_ref, ahead, stat_in, ka.at[odd], va.at[odd]),
        )
        dkv_ref[h, 0] = (scale * ka[odd]).astype(BF16)
        dkv_ref[h, 1] = va[odd].astype(BF16)

    def head(h):
        near_copy(h).wait()
        for j in range(4):
            halo_copy(h, j).wait_recv()
        for k in range(n - 1):
            far_copy(h, k).wait_recv()
            follow(h + 1, k)

        odd = lax.rem(h, 2)

        def move(i):
            for s in range(LIVE):
                cur[i * LIVE + s] = recv[h, i, s]

        over(0, n, move)
        kx[:WINDOW, :] = halo[h, 0]
        kx[WINDOW:, :] = own_ref[h, 0]
        vx[:WINDOW, :] = halo[h, 1]
        vx[WINDOW:, :] = own_ref[h, 1]
        ka[odd] = jnp.zeros_like(ka[odd])
        va[odd] = jnp.zeros_like(va[odd])

        def tile(t):
            refs = (
                plan_s, qg_ref, o_ref, dq_ref, stat, cur,
                kx, vx, km, vm, s_ref, dp_ref, p_ref, ds_ref,
            )
            attend_tile(refs, t, me, h, ka.at[odd], va.at[odd])

        over(0, tiles, tile)
        stat_copy(h).start()

        @pl.when(h > 0)
        def _():
            finish(h - 1)

    over(0, heads, head)
    finish(heads - 1)

    over(1, m, lambda r: tab_near(r).wait_send())
    over(1, n, lambda r: tab_far(r).wait_send())

    each_part(lambda h, j: halo_copy(h, j).wait_send())
    each_part(lambda h, j: ahead_copy(h, j).wait_send())

    def drain(h):
        stat_copy(h).wait_send()
        for k in range(n - 1):
            far_copy(h, k).wait_send()

    over(0, heads, drain)


def exchange(ids, used, q, g, k, v, mem_k, mem_v, heads, n, m):
    rows = q.shape[0]
    tokens = rows // heads
    tiles = tokens // TILE
    span = WINDOW + TILE
    total = span + TOPK * BLOCK
    halves = TILE // BLOCK
    pairs = heads * tiles * total * TILE
    vmem = pl.BlockSpec(memory_space=pltpu.VMEM)
    smem = pl.BlockSpec(memory_space=pltpu.SMEM)
    hbm = pl.BlockSpec(memory_space=pl.ANY)
    dma = pltpu.SemaphoreType.DMA
    by_head = (heads, tokens, 128)
    by_pair = (heads, 2, tokens, 128)
    return pl.pallas_call(
        functools.partial(exchange_body, heads, n, m),
        in_specs=[smem, smem] + [hbm] * 6,
        out_specs=[vmem, vmem, vmem],
        out_shape=[
            jax.ShapeDtypeStruct(by_head, BF16),
            jax.ShapeDtypeStruct(by_head, BF16),
            jax.ShapeDtypeStruct(by_pair, BF16),
        ],
        scratch_shapes=[
            pltpu.VMEM((4, rows, 128), BF16),
            pltpu.VMEM((2,) + mem_k.shape, BF16),
            pltpu.VMEM(by_pair, BF16),
            pltpu.VMEM(by_pair, BF16),
            pltpu.VMEM((heads, n, LIVE, 2, BLOCK, 128), BF16),
            pltpu.VMEM((m, 8, 128), jnp.int32),
            pltpu.VMEM((8, 128), jnp.int32),
            pltpu.VMEM((n, 8, 128), jnp.int32),
            pltpu.VMEM((n, 128), jnp.int32),
            pltpu.VMEM((LIVE + 1, n, 128), jnp.int32),
            pltpu.SMEM((LIVE + 1, n, 128), jnp.int32),
            pltpu.VMEM((heads, n, LIVE, 2, BLOCK, 128), BF16),
            pltpu.VMEM(by_pair, BF16),
            pltpu.VMEM(by_pair, BF16),
            pltpu.VMEM((heads, tiles, 8, TILE), F32),
            pltpu.VMEM((heads, tiles, 8, TILE), F32),
            pltpu.VMEM((n * LIVE, 2, BLOCK, 128), BF16),
            pltpu.VMEM((2 * WINDOW, 128), BF16),
            pltpu.VMEM((2 * WINDOW, 128), BF16),
            pltpu.VMEM((halves, TOPK * BLOCK, 128), BF16),
            pltpu.VMEM((halves, TOPK * BLOCK, 128), BF16),
            pltpu.VMEM((total, TILE), F32),
            pltpu.VMEM((total, TILE), F32),
            pltpu.VMEM((total, TILE), BF16),
            pltpu.VMEM((total, TILE), BF16),
            pltpu.VMEM((2, WINDOW, 128), F32),
            pltpu.VMEM((2, WINDOW, 128), F32),
            dma((6,)), dma, dma((m,)), dma((m,)), dma((n,)), dma((n,)),
            dma((heads, n)), dma((heads, n)), dma((heads,)),
            dma((heads, 4)), dma((heads, 4)), dma((heads, 4)), dma((heads, 4)),
            dma((heads,)), dma((heads,)),
        ],
        compiler_params=pltpu.CompilerParams(
            vmem_limit_bytes=VMEM, collective_id=0, has_side_effects=True
        ),
        cost_estimate=pl.CostEstimate(
            flops=pairs * 128 * 12, bytes_accessed=heads * 6 * 2**20, transcendentals=pairs
        ),
        name="exchange_attend",
    )(ids, used, q, g, k, v, mem_k, mem_v)


def join_body(heads, o_ref, dq_ref, dkv_ref, o_out, dq_out, dk_out, dv_out):
    perm = heads_to_rows(256, heads)
    per = 256 // heads
    for part in range(o_out.shape[0] // 256):
        src = slice(part * per, (part + 1) * per)
        dst = slice(part * 256, (part + 1) * 256)
        o = jnp.concatenate([o_ref[h, src, :] for h in range(heads)], 0)
        dq = jnp.concatenate([dq_ref[h, src, :] for h in range(heads)], 0)
        both = dot(perm, jnp.concatenate([o, dq], 1)).astype(BF16)
        o_out[dst, :] = both[:, :128]
        dq_out[dst, :] = both[:, 128:]
        dk = jnp.concatenate([dkv_ref[h, 0, src, :] for h in range(heads)], 0)
        dv = jnp.concatenate([dkv_ref[h, 1, src, :] for h in range(heads)], 0)
        both = dot(perm, jnp.concatenate([dk, dv], 1)).astype(BF16)
        dk_out[dst, :] = both[:, :128]
        dv_out[dst, :] = both[:, 128:]


def join_heads(o, dq, dkv):
    heads, tokens = o.shape[:2]
    steps = 4
    hm = pl.BlockSpec((heads, tokens // steps, 128), lambda i: (0, i, 0))
    kv = pl.BlockSpec((heads, 2, tokens // steps, 128), lambda i: (0, 0, i, 0))
    out = pl.BlockSpec((tokens * heads // steps, 128), lambda i: (i, 0))
    return pl.pallas_call(
        functools.partial(join_body, heads),
        grid=(steps,),
        in_specs=[hm, hm, kv],
        out_specs=[out] * 4,
        out_shape=[jax.ShapeDtypeStruct((tokens * heads, 128), BF16)] * 4,
        compiler_params=pltpu.CompilerParams(vmem_limit_bytes=VMEM),
        cost_estimate=pl.CostEstimate(
            flops=4 * 2 * tokens * heads * 256 * 128,
            bytes_accessed=16 * tokens * heads * 128,
            transcendentals=0,
        ),
        name="join_heads",
    )(o, dq, dkv)


def shards(queries, seg_keys, seg_values, mem_keys, mem_values, mem_blocks, mem_count, grad_out):
    tokens, heads, dim = queries.shape
    mem_local = mem_keys.shape[0] // BLOCK

    def as_rows(x):
        return x.reshape(x.shape[0] * heads, dim)

    def as_blocks(x):
        return x.reshape(mem_local, BLOCK * heads, dim)

    outs = exchange(
        mem_blocks, mem_count,
        as_rows(queries), as_rows(grad_out), as_rows(seg_keys), as_rows(seg_values),
        as_blocks(mem_keys), as_blocks(mem_values),
        heads, lax.axis_size("seq"), lax.axis_size("head"),
    )
    return tuple(x.reshape(tokens, heads, dim) for x in join_heads(*outs))


def solution(mesh):
    wide = P("seq", "head", None)
    return jax.shard_map(
        shards,
        mesh=mesh,
        in_specs=(wide, wide, wide, wide, wide, P(("seq", "head"), None), P(("seq", "head")), wide),
        out_specs=(wide, wide, wide, wide),
        check_vma=False,
    )
```
